32 devices in a mesh: lon: 2 (over x), lat: 4 (over y, core), lev: 4 (over z).
Axes of the slice: x: 2, y: 2, z: 4, core: 2. Of those that a mesh axis runs over, the one named last changes fastest.
Arguments:
- fields: float32 [3, 8, 60, 512], P(None, 'lev', 'lon', 'lat'), may hold values from -6 to 6
- spectral_coeffs: float32 [3, 8], P(None, 'lev'), may hold values from 0.3 to 3
- mlp_in: bfloat16 [384, 24], replicated, may hold values from -1.25 to 1.25
- mlp_mid: bfloat16 [2, 384, 384], replicated, may hold values from -0.3125 to 0.3125
- mlp_out: bfloat16 [24, 384], replicated, may hold values from -0.3125 to 0.3125
Outputs:
- updated: float32 [3, 8, 60, 512], P(None, 'lev', 'lon', 'lat')
The draws below stay inside these ranges and needn't reach their ends.
All inputs are finite; a program needn't handle non-finite values.
Results may differ from the reference program's by a relative error of at most 0.0012.
Values may be sent and summed in bfloat16 or wider, within the bound.
No kernel may reach another device: no remote copies, remote signals or barrier semaphores. Data moves between devices by JAX's collectives and lax.ppermute only.
A program may use at most 64 MiB of HBM per device.

```python
import math
import jax
import jax.numpy as jnp
from jax import lax

WAVES = 320
KMAX = 320
UNITS = 384
SUBSTEPS = 2
NLON = 60
NLAT = 512
LEVELS = 8


def block_levels(stream_key, dims, shards, low, largest):
    factor_of, own = 1.0, jax.random.fold_in(stream_key, 6)
    for position, blocks in shards:
        steps = jnp.exp(jax.random.uniform(jax.random.fold_in(own, position), (blocks,), jnp.float32, low / len(shards), largest / len(shards)))
        factor_of = factor_of * jnp.repeat(steps, dims[position] // blocks).reshape([-1 if axis == position else 1 for axis in range(len(dims))])
    return factor_of


def bell_draw(stream_key, shape, scale, reach, pieces=(), kind=jnp.bfloat16):
    factor_of = block_levels(stream_key, shape, pieces, -0.22, 0.18) if pieces else 1.0
    array = jax.random.normal(stream_key, shape, jnp.float32) * scale * factor_of
    return jnp.minimum(jnp.maximum(array, -reach), reach).astype(kind)


def setup_inputs(seed: int = 0) -> dict:
    key_of = jax.random.split(jax.random.key(seed), 6)
    return {
        "fields": bell_draw(key_of[0], (3, LEVELS, NLON, NLAT), 1.0, 6.0, ((1, 4), (2, 2), (3, 4)), jnp.float32),
        "spectral_coeffs": jnp.clip(jnp.exp(math.log(3.0) - 2.3025851 * jax.random.uniform(key_of[1], (3, LEVELS), jnp.float32) ** block_levels(key_of[1], (3, LEVELS), ((1, 4),), -0.2, 0.2)), 0.3, 3.0),
        "mlp_in": bell_draw(key_of[2], (UNITS, 3 * LEVELS), (3 * LEVELS) ** -0.5, 1.25),
        "mlp_mid": bell_draw(key_of[3], (2, UNITS, UNITS), UNITS ** -0.5, 0.3125),
        "mlp_out": bell_draw(key_of[4], (3 * LEVELS, UNITS), UNITS ** -0.5, 0.3125),
    }


highest = lax.Precision.HIGHEST


def forward_table(lon_ids, total_lon, waves):
    wave_ids = jnp.arange(waves, dtype=jnp.int32)
    phase = ((lon_ids[:, None] * wave_ids[None, :]) % total_lon).astype(jnp.float32) * (2.0 * jnp.pi / total_lon)
    return jnp.concatenate([jnp.cos(phase), -jnp.sin(phase)], axis=1) / total_lon


def inverse_table(lon_ids, total_lon, waves):
    wave_ids = jnp.arange(waves, dtype=jnp.int32)
    phase = ((wave_ids[:, None] * lon_ids[None, :]) % total_lon).astype(jnp.float32) * (2.0 * jnp.pi / total_lon)
    weight = jnp.where(wave_ids == 0, 1.0, 2.0).astype(jnp.float32)[:, None]
    return jnp.concatenate([weight * jnp.cos(phase), -weight * jnp.sin(phase)], axis=0)


def latitude_tables(lat_ids, total_lat, degree_ids):
    odd_rows = 2 * lat_ids[:, None] + 1
    period = 4 * total_lat
    scale = jnp.pi / (2.0 * total_lat)
    even_arg = ((odd_rows * degree_ids[None, :]) % period).astype(jnp.float32) * scale
    odd_arg = ((odd_rows * (degree_ids[None, :] + 1)) % period).astype(jnp.float32) * scale
    return jnp.cos(even_arg), jnp.sin(odd_arg)


def latitude_forward(waves, even_tab, odd_tab):
    cols, nf, levs, lats = waves.shape
    pairs = waves.reshape(cols // 2, 2, nf, levs, lats)
    even_part = jnp.einsum("pfli,ik->pflk", pairs[:, 0], even_tab, precision=highest)
    odd_part = jnp.einsum("pfli,ik->pflk", pairs[:, 1], odd_tab, precision=highest)
    return jnp.stack([even_part, odd_part], axis=1).reshape(cols, nf, levs, even_tab.shape[1])


def latitude_inverse(spectra, even_tab, odd_tab):
    cols, nf, levs, degs = spectra.shape
    pairs = spectra.reshape(cols // 2, 2, nf, levs, degs)
    even_part = jnp.einsum("pflk,ik->pfli", pairs[:, 0], even_tab, precision=highest)
    odd_part = jnp.einsum("pflk,ik->pfli", pairs[:, 1], odd_tab, precision=highest)
    return jnp.stack([even_part, odd_part], axis=1).reshape(cols, nf, levs, even_tab.shape[0])


def operator(spectra, coeffs, col_waves, degree_ids):
    parity = col_waves % 2
    freq = (degree_ids[None, :] + parity[:, None]).astype(jnp.float32)
    wavenum = col_waves.astype(jnp.float32)[:, None]
    qvalue = ((wavenum * wavenum + freq * freq) / (KMAX * KMAX))[:, None, :]
    hyper = coeffs[0][None, :, None]
    coupling = coeffs[1][None, :, None]
    depth = coeffs[2][None, :, None]
    vort = spectra[:, 0]
    diverg = spectra[:, 1]
    temper = spectra[:, 2]
    new_vort = vort / (1.0 + hyper * qvalue * qvalue)
    new_div = (diverg + coupling * qvalue * temper) / (1.0 + coupling * depth * qvalue)
    new_temp = temper - depth * new_div
    return jnp.stack([new_vort - vort, new_div - diverg, new_temp - temper], axis=1)


def nonlinear(state):
    temper = state[2] + 0.25 * state[0] * state[1]
    return jnp.stack([state[0], state[1], temper], axis=0)


def reference(fields, spectral_coeffs, mlp_in, mlp_mid, mlp_out):
    nf, levels, total_lon, total_lat = fields.shape
    lon_ids = jnp.arange(total_lon, dtype=jnp.int32)
    fwd_tab = forward_table(lon_ids, total_lon, WAVES)
    inv_tab = inverse_table(lon_ids, total_lon, WAVES)
    even_tab, odd_tab = latitude_tables(jnp.arange(total_lat, dtype=jnp.int32), total_lat, jnp.arange(KMAX, dtype=jnp.int32))
    weight = 2.0 / total_lat
    col_waves = jnp.arange(2 * WAVES, dtype=jnp.int32) % WAVES
    degree_ids = jnp.arange(KMAX, dtype=jnp.int32)
    state = fields
    for substep in range(SUBSTEPS):
        waves = jnp.einsum("flji,jc->cfli", state, fwd_tab, precision=highest)
        spectra = latitude_forward(waves, even_tab * weight, odd_tab * weight)
        change = operator(spectra, spectral_coeffs, col_waves, degree_ids)
        back = latitude_inverse(change, even_tab, odd_tab)
        increment = jnp.einsum("cfli,cj->flji", back, inv_tab, precision=highest)
        state = nonlinear(state + increment)

    def column_block(block):
        inputs = block.astype(jnp.bfloat16).reshape(nf * levels, total_lat)
        hidden = jax.nn.silu(jnp.dot(mlp_in, inputs, preferred_element_type=jnp.float32)).astype(jnp.bfloat16)
        hidden = jax.nn.silu(jnp.dot(mlp_mid[0], hidden, preferred_element_type=jnp.float32)).astype(jnp.bfloat16)
        hidden = jax.nn.silu(jnp.dot(mlp_mid[1], hidden, preferred_element_type=jnp.float32)).astype(jnp.bfloat16)
        output = jnp.dot(mlp_out, hidden, preferred_element_type=jnp.float32).astype(jnp.bfloat16)
        return output.reshape(nf, levels, total_lat)

    correction = lax.map(column_block, state.transpose(2, 0, 1, 3)).transpose(1, 2, 0, 3)
    return state + correction.astype(jnp.float32)
```

```python
import functools

import jax
import jax.numpy as jnp
import numpy as np
from jax import lax
from jax.experimental import pallas as pl
from jax.experimental.pallas import tpu as pltpu
from jax.sharding import PartitionSpec as P

WAVES = 320
KMAX = 320
SUBSTEPS = 2


highest = lax.Precision.HIGHEST
LANES = 128
PLANE_LIMIT = 4 * 1024 * 1024


def round_up(value, unit):
    return -(-value // unit) * unit


def forward_table(lon_ids, total_lon, waves):
    wave_ids = jnp.arange(waves, dtype=jnp.int32)
    phase = (lon_ids[:, None] * wave_ids[None, :] % total_lon).astype(jnp.float32) * (
        2.0 * jnp.pi / total_lon
    )
    return jnp.concatenate([jnp.cos(phase), -jnp.sin(phase)], axis=1) / total_lon


def inverse_table(lon_ids, total_lon, waves):
    wave_ids = jnp.arange(waves, dtype=jnp.int32)
    phase = (wave_ids[:, None] * lon_ids[None, :] % total_lon).astype(jnp.float32) * (
        2.0 * jnp.pi / total_lon
    )
    weight = jnp.where(wave_ids == 0, 1.0, 2.0).astype(jnp.float32)[:, None]
    return jnp.concatenate([weight * jnp.cos(phase), -weight * jnp.sin(phase)], axis=0)


def latitude_tables(lat_ids, total_lat, degree_ids):
    odd_rows = 2 * lat_ids[:, None] + 1
    period = 4 * total_lat
    scale = jnp.pi / (2.0 * total_lat)
    even_arg = (odd_rows * degree_ids[None, :] % period).astype(jnp.float32) * scale
    odd_arg = (odd_rows * (degree_ids[None, :] + 1) % period).astype(jnp.float32) * scale
    return (jnp.cos(even_arg), jnp.sin(odd_arg))


def latitude_forward(waves, even_tab, odd_tab):
    cols, nf, levs, lats = waves.shape
    pairs = waves.reshape(cols // 2, 2, nf, levs, lats)
    even_part = jnp.einsum("pfli,ik->pflk", pairs[:, 0], even_tab, precision=highest)
    odd_part = jnp.einsum("pfli,ik->pflk", pairs[:, 1], odd_tab, precision=highest)
    return jnp.stack([even_part, odd_part], axis=1).reshape(cols, nf, levs, even_tab.shape[1])


def latitude_inverse(spectra, even_tab, odd_tab):
    cols, nf, levs, degs = spectra.shape
    pairs = spectra.reshape(cols // 2, 2, nf, levs, degs)
    even_part = jnp.einsum("pflk,ik->pfli", pairs[:, 0], even_tab, precision=highest)
    odd_part = jnp.einsum("pflk,ik->pfli", pairs[:, 1], odd_tab, precision=highest)
    return jnp.stack([even_part, odd_part], axis=1).reshape(cols, nf, levs, even_tab.shape[0])


def operator(spectra, coeffs, col_waves, degree_ids):
    parity = col_waves % 2
    freq = (degree_ids[None, :] + parity[:, None]).astype(jnp.float32)
    wavenum = col_waves.astype(jnp.float32)[:, None]
    qvalue = ((wavenum * wavenum + freq * freq) / (KMAX * KMAX))[:, None, :]
    hyper = coeffs[0][None, :, None]
    coupling = coeffs[1][None, :, None]
    depth = coeffs[2][None, :, None]
    vort = spectra[:, 0]
    diverg = spectra[:, 1]
    temper = spectra[:, 2]
    new_vort = vort / (1.0 + hyper * qvalue * qvalue)
    new_div = (diverg + coupling * qvalue * temper) / (1.0 + coupling * depth * qvalue)
    new_temp = temper - depth * new_div
    return jnp.stack([new_vort - vort, new_div - diverg, new_temp - temper], axis=1)


def nonlinear(state):
    temper = state[2] + 0.25 * state[0] * state[1]
    return jnp.stack([state[0], state[1], temper], axis=0)


def transposing(fields, spectral_coeffs, mlp_in, mlp_mid, mlp_out):
    nf, lev_dev, lon_dev, lat_dev = fields.shape
    lon_count = lax.axis_size("lon")
    lat_count = lax.axis_size("lat")
    total_lon = lon_dev * lon_count
    total_lat = lat_dev * lat_count
    wave_cols = 2 * WAVES // lon_count
    row_count = nf * lev_dev * lat_dev
    lat_ids = lax.axis_index("lat") * lat_dev + jnp.arange(lat_dev, dtype=jnp.int32)
    col_waves = (lax.axis_index("lon") * wave_cols + jnp.arange(wave_cols, dtype=jnp.int32)) % WAVES
    weight = 2.0 / total_lat
    all_lons = jnp.arange(total_lon, dtype=jnp.int32)
    fwd_full = forward_table(all_lons, total_lon, WAVES)
    inv_full = inverse_table(all_lons, total_lon, WAVES)
    own_degrees = jnp.arange(KMAX, dtype=jnp.int32)
    full_even, full_odd = latitude_tables(lat_ids, total_lat, own_degrees)
    state = fields
    for substep in range(SUBSTEPS):
        flat = state.transpose(0, 1, 3, 2).reshape(row_count, lon_dev)
        by_row = lax.all_to_all(flat, "lon", split_axis=0, concat_axis=1, tiled=True)
        row_waves = jnp.dot(by_row, fwd_full, precision=highest)
        by_col = lax.all_to_all(row_waves, "lon", split_axis=1, concat_axis=0, tiled=True)
        waves = by_col.reshape(nf, lev_dev, lat_dev, wave_cols).transpose(3, 0, 1, 2)
        partial_spectra = latitude_forward(waves, full_even * weight, full_odd * weight)
        spectra = lax.psum(partial_spectra, "lat")
        change = operator(spectra, spectral_coeffs, col_waves, own_degrees)
        back = latitude_inverse(change, full_even, full_odd)
        flat_back = back.transpose(1, 2, 3, 0).reshape(row_count, wave_cols)
        full_waves = lax.all_to_all(flat_back, "lon", split_axis=0, concat_axis=1, tiled=True)
        row_grid = jnp.dot(full_waves, inv_full, precision=highest)
        own_grid = lax.all_to_all(row_grid, "lon", split_axis=1, concat_axis=0, tiled=True)
        increment = own_grid.reshape(nf, lev_dev, lat_dev, lon_dev).transpose(0, 1, 3, 2)
        state = nonlinear(state + increment)
    features = state.astype(jnp.bfloat16).reshape(nf, lev_dev, lon_dev * lat_dev)
    columns = lax.all_to_all(features, "lev", split_axis=2, concat_axis=1, tiled=True)
    levels = columns.shape[1]
    inputs = columns.reshape(nf * levels, columns.shape[2])
    hidden = jax.nn.silu(jnp.dot(mlp_in, inputs, preferred_element_type=jnp.float32)).astype(
        jnp.bfloat16
    )
    hidden = jax.nn.silu(jnp.dot(mlp_mid[0], hidden, preferred_element_type=jnp.float32)).astype(
        jnp.bfloat16
    )
    hidden = jax.nn.silu(jnp.dot(mlp_mid[1], hidden, preferred_element_type=jnp.float32)).astype(
        jnp.bfloat16
    )
    output = jnp.dot(mlp_out, hidden, preferred_element_type=jnp.float32).astype(jnp.bfloat16)
    output = output.reshape(nf, levels, columns.shape[2])
    returned = lax.all_to_all(output, "lev", split_axis=1, concat_axis=2, tiled=True)
    return state + returned.astype(jnp.float32).reshape(state.shape)


class Plan:
    def __init__(self, mesh_shape, local):
        self.nf, self.levs, self.lon_dev, self.lat_dev = local
        self.lons = mesh_shape["lon"]
        self.lats = mesh_shape["lat"]
        self.zs = mesh_shape["lev"]
        self.n_lon = self.lons * self.lon_dev
        self.n_lat = self.lats * self.lat_dev
        self.jpad = round_up(self.lon_dev, 16)
        self.rows = self.lons * self.jpad
        classes = min(self.n_lon // 2 + 1, WAVES)
        self.half = round_up((classes + 1) // 2, 16)
        self.block = 2 * self.half
        self.modes = 2 * self.block
        self.degs = round_up(KMAX, LANES)
        self.feats = round_up(self.nf * self.levs, 8)

    def fits(self):
        plane = self.nf * self.levs * self.n_lon * self.n_lat * 4
        power_of_two = all(n & (n - 1) == 0 for n in (self.lons, self.lats, self.zs))
        return (
            SUBSTEPS == 2
            and self.nf == 3
            and power_of_two
            and plane <= PLANE_LIMIT
            and self.n_lon % 2 == 0
            and self.lat_dev % LANES == 0
            and KMAX < self.n_lat
        )


def split_np(table):
    high = table.astype(np.float32).astype(jnp.bfloat16)
    low = (table - high.astype(np.float64)).astype(jnp.bfloat16)
    return high, low


def zonal_tables(plan):
    lon = np.arange(plan.n_lon)
    pos = (lon // plan.lon_dev) * plan.jpad + lon % plan.lon_dev
    ana = np.zeros((plan.modes, plan.rows))
    syn = np.zeros((plan.rows, plan.modes))
    classes = min(plan.n_lon // 2 + 1, WAVES)
    for rho in range(classes):
        phase = 2.0 * np.pi * ((rho * lon) % plan.n_lon) / plan.n_lon
        cos_row = (rho % 2) * plan.block + rho // 2
        ana[cos_row, pos] = np.cos(phase) / plan.n_lon
        syn[pos, cos_row] = np.cos(phase)
        if rho > 0 and 2 * rho != plan.n_lon:
            ana[cos_row + plan.half, pos] = -np.sin(phase) / plan.n_lon
            syn[pos, cos_row + plan.half] = -np.sin(phase)
    ana_h, ana_l = split_np(ana)
    syn_h, syn_l = split_np(syn)
    return (
        np.concatenate([ana_h, ana_l, ana_h], axis=1),
        np.concatenate([syn_h, syn_l, syn_h], axis=1),
    )


def meridional_tables(plan):
    lat = np.arange(plan.n_lat)[:, None]
    deg = np.arange(KMAX)[None, :]
    period = 4 * plan.n_lat
    scale = np.pi / (2.0 * plan.n_lat)
    even = np.cos(((2 * lat + 1) * deg % period) * scale)
    odd = np.sin(((2 * lat + 1) * (deg + 1) % period) * scale)
    out = np.zeros((2, 2, plan.n_lat, plan.degs), dtype=jnp.bfloat16)
    for parity, table in enumerate((even, odd)):
        high, low = split_np(table)
        out[parity, 0, :, :KMAX] = high
        out[parity, 1, :, :KMAX] = low
    return out


def split(value):
    high = value.astype(jnp.bfloat16)
    low = (value - high.astype(jnp.float32)).astype(jnp.bfloat16)
    return high, low


def mm(left, right):
    return lax.dot_general(
        left, right, (((1,), (0,)), ((), ())), preferred_element_type=jnp.float32
    )


def mm_t(left, right):
    return lax.dot_general(
        left, right, (((1,), (1,)), ((), ())), preferred_element_type=jnp.float32
    )


def prepare_kernel(plan, pos_ref, coef_ref, win_ref, wout_ref, sv_ref, sq_ref, w1_ref, wo_ref):
    row = lax.broadcasted_iota(jnp.int32, (plan.half, plan.degs), 0)
    deg = lax.broadcasted_iota(jnp.int32, (plan.half, plan.degs), 1)
    inv_k2 = 1.0 / (KMAX * KMAX)
    for parity in range(2):
        rho = 2 * row + parity
        freq = (deg + parity).astype(jnp.float32)
        freq2 = freq * freq
        sums = [[jnp.zeros((plan.half, plan.degs), jnp.float32) for _ in range(2)] for _ in range(plan.levs)]
        turns = -(-WAVES // plan.n_lon)
        terms = [(rho + plan.n_lon * a, rho >= 0) for a in range(turns)]
        terms += [(plan.n_lon * (a + 1) - rho, rho > 0) for a in range(turns)]
        for number, (wave, extra) in enumerate(terms):
            valid = (wave < WAVES) & extra & (2 * rho <= plan.n_lon)
            if number >= turns:
                valid = valid & (2 * rho != plan.n_lon)
            weight = jnp.where(valid, jnp.where(wave == 0, 1.0, 2.0), 0.0)
            wavef = wave.astype(jnp.float32)
            q = (wavef * wavef + freq2) * inv_k2
            for lev in range(plan.levs):
                nu, ga, gb = (coef_ref[i, lev] for i in range(3))
                hyper = nu * q * q
                wave_q = ga * q
                sums[lev][0] -= weight * (hyper / (1.0 + hyper))
                sums[lev][1] += weight * (wave_q / (1.0 + gb * wave_q))
        for lev in range(plan.levs):
            sv_ref[lev, parity] = sums[lev][0]
            sq_ref[lev, parity] = sums[lev][1]
    own_z = pos_ref[2]
    total = plan.zs * plan.levs
    nin = plan.nf * total

    def feature_of(slot):
        block = slot // plan.feats
        inner = slot % plan.feats
        field = inner // plan.levs
        level = (own_z ^ block) * plan.levs + inner % plan.levs
        return jnp.where(inner < plan.nf * plan.levs, field * total + level, -1)

    wide = plan.zs * plan.feats
    source = lax.broadcasted_iota(jnp.int32, (nin, wide), 0)
    slot = lax.broadcasted_iota(jnp.int32, (nin, wide), 1)
    pick = (source == feature_of(slot)).astype(jnp.float32).astype(jnp.bfloat16)
    w1_ref[...] = (0.5 * mm(win_ref[...], pick)).astype(jnp.bfloat16)
    slot = lax.broadcasted_iota(jnp.int32, (plan.feats, nin), 0)
    source = lax.broadcasted_iota(jnp.int32, (plan.feats, nin), 1)
    pick = (source == feature_of(slot)).astype(jnp.float32).astype(jnp.bfloat16)
    wo_ref[...] = mm(pick, wout_ref[...]).astype(jnp.bfloat16)


def prepare(plan, pos, coeffs, mlp_in, mlp_out):
    units = mlp_in.shape[0]
    table = jax.ShapeDtypeStruct((plan.levs, 2, plan.half, plan.degs), jnp.float32)
    smem = pl.BlockSpec(memory_space=pltpu.SMEM)
    vmem = pl.BlockSpec(memory_space=pltpu.VMEM)
    return pl.pallas_call(
        functools.partial(prepare_kernel, plan),
        out_shape=(
            table,
            table,
            jax.ShapeDtypeStruct((units, plan.zs * plan.feats), jnp.bfloat16),
            jax.ShapeDtypeStruct((plan.feats, units), jnp.bfloat16),
        ),
        in_specs=[smem, smem, vmem, vmem],
        out_specs=(vmem,) * 4,
        compiler_params=pltpu.CompilerParams(vmem_limit_bytes=16 * 1024 * 1024),
        name="prepare",
    )(pos, coeffs, mlp_in, mlp_out)


def dynamics_kernel(plan, blocks, *refs):
    pos_ref, coef_ref = refs[:2]
    block_refs = refs[2 : 2 + blocks]
    ana_ref, syn_ref, mer_ref, sv_ref, sq_ref = refs[2 + blocks : 7 + blocks]
    state_ref, feat_ref = refs[7 + blocks : 9 + blocks]
    grid_ref, wh_ref, wl_ref, prod_ref, tile_ref = refs[9 + blocks :]
    own_lon, own_lat = pos_ref[0], pos_ref[1]
    nf, levs, lats = plan.nf, plan.levs, plan.lats
    block, half = plan.block, plan.half
    if plan.jpad != plan.lon_dev:
        tail = (plan.lon_dev // 8) * 8
        for lon in range(plan.lons):
            start = lon * plan.jpad + tail
            stop = (lon + 1) * plan.jpad
            for lat in range(lats):
                for f in range(nf):
                    for l in range(levs):
                        grid_ref[lat, f, l, start:stop, :] = jnp.zeros((stop - start, plan.lat_dev), jnp.float32)
    for s in range(blocks):
        lon = own_lon ^ (s % plan.lons)
        lat = own_lat ^ (s // plan.lons)
        row = pl.multiple_of(lon * plan.jpad, 8)
        for f in range(nf):
            for l in range(levs):
                grid_ref[lat, f, l, pl.ds(row, plan.lon_dev), :] = block_refs[s][f, l]

    def whole(ref, *index):
        return jnp.concatenate([ref[(lat, *index)] for lat in range(lats)], axis=1)

    def analyse(values):
        for n, value in enumerate(values):
            high, low = split(value)
            waves = mm(ana_ref[...], jnp.concatenate([high, high, low], axis=0))
            high, low = split(waves)
            for parity in range(2):
                rows = slice(parity * block, (parity + 1) * block)
                wh_ref[parity, n * block : (n + 1) * block, :] = high[rows]
                wl_ref[parity, n * block : (n + 1) * block, :] = low[rows]
        size = len(values) * block
        weight = 2.0 / plan.n_lat
        out = []
        for parity in range(2):
            high, low = wh_ref[parity, :size, :], wl_ref[parity, :size, :]
            total = mm(high, mer_ref[parity, 0]) + mm(low, mer_ref[parity, 0]) + mm(high, mer_ref[parity, 1])
            out.append(total * weight)
        return out

    def synthesise(spectra, rows, tables, width):
        parts = []
        for parity in range(2):
            high, low = split(spectra[parity])
            thigh, tlow = tables[parity]
            parts.append(mm_t(high, thigh) + mm_t(low, thigh) + mm_t(high, tlow))
        count = spectra[0].shape[0] // block
        out = []
        for n in range(count):
            both = jnp.concatenate([part[n * block : (n + 1) * block] for part in parts], axis=0)
            high, low = split(both)
            out.append(mm(rows, jnp.concatenate([high, high, low], axis=0)))
        return out

    def at(spectrum, f, l):
        n = f * levs + l
        return spectrum[n * block : (n + 1) * block]

    deg = lax.broadcasted_iota(jnp.int32, (block, plan.degs), 1)
    cls = lax.broadcasted_iota(jnp.int32, (block, plan.degs), 0) % half
    norms, counts = [], []
    for parity in range(2):
        rho = 2 * cls + parity
        alone = (rho == 0) | (2 * rho == plan.n_lon)
        norm = jnp.where(alone, 1.0, 0.5)
        norms.append(norm * jnp.where(deg == 0, 2.0, 1.0) if parity == 0 else norm)
        weight = jnp.zeros((block, plan.degs), jnp.float32)
        for a in range(-(-WAVES // plan.n_lon)):
            wave = rho + plan.n_lon * a
            weight += jnp.where(wave < WAVES, jnp.where(wave == 0, 1.0, 2.0), 0.0)
            wave = plan.n_lon * (a + 1) - rho
            weight += jnp.where((wave < WAVES) & (rho > 0) & (2 * rho < plan.n_lon), 2.0, 0.0)
        counts.append(weight)

    def changes(spectra):
        out = []
        for parity in range(2):
            per = [[None] * levs for _ in range(nf)]
            for l in range(levs):
                sv = jnp.concatenate([sv_ref[l, parity]] * 2, axis=0)
                sq = jnp.concatenate([sq_ref[l, parity]] * 2, axis=0)
                gb = coef_ref[2, l]
                vort, diverg, temper = (spectra[parity][f][l] for f in range(3))
                per[0][l] = sv * vort
                per[1][l] = sq * (temper - gb * diverg)
                per[2][l] = -gb * (counts[parity] * diverg + per[1][l])
            out.append(per)
        return out

    def stack(nested, fields):
        return [
            jnp.concatenate([nested[parity][f][l] for f in fields for l in range(levs)], axis=0)
            for parity in range(2)
        ]

    flat = analyse([whole(grid_ref, f, l) for f in range(nf) for l in range(levs)])
    spectra = [[[at(flat[parity], f, l) for l in range(levs)] for f in range(nf)] for parity in range(2)]
    first = changes(spectra)
    full = [(mer_ref[parity, 0], mer_ref[parity, 1]) for parity in range(2)]
    grown = synthesise(stack(first, (0, 1)), syn_ref[...], full, plan.n_lat)
    products = []
    for l in range(levs):
        vort = whole(grid_ref, 0, l) + grown[l]
        diverg = whole(grid_ref, 1, l) + grown[levs + l]
        product = 0.25 * vort * diverg
        products.append(product)
        for lat in range(lats):
            prod_ref[lat, l] = product[:, lat * plan.lat_dev : (lat + 1) * plan.lat_dev]
    extra = analyse(products)
    updated = []
    for parity in range(2):
        per = [
            [spectra[parity][f][l] + norms[parity] * first[parity][f][l] for l in range(levs)] for f in range(nf)
        ]
        per[2] = [per[2][l] + at(extra[parity], 0, l) for l in range(levs)]
        updated.append(per)
    second = changes(updated)
    both = [
        [[first[parity][f][l] + second[parity][f][l] for l in range(levs)] for f in range(nf)] for parity in range(2)
    ]
    own_start = pl.multiple_of(own_lat * plan.lat_dev, LANES)
    own_row = pl.multiple_of(own_lon * plan.jpad, 8)
    own_tables = [
        tuple(mer_ref[parity, part, pl.ds(own_start, plan.lat_dev), :] for part in range(2)) for parity in range(2)
    ]
    own = synthesise(
        stack(both, range(nf)), syn_ref[pl.ds(own_row, plan.jpad), :], own_tables, plan.lat_dev
    )
    if plan.feats != nf * levs:
        tile_ref[...] = jnp.zeros(tile_ref.shape, jnp.float32)
    for l in range(levs):
        vort, diverg, temper = (
            grid_ref[own_lat, f, l, pl.ds(own_row, plan.jpad), :] + own[f * levs + l] for f in range(3)
        )
        temper = temper + prod_ref[own_lat, l, pl.ds(own_row, plan.jpad), :] + 0.25 * vort * diverg
        for f, value in enumerate((vort, diverg, temper)):
            state_ref[f, l] = value[: plan.lon_dev]
            tile_ref[:, f * levs + l, :] = value[: plan.lon_dev]
    feat_ref[...] = tile_ref[...].astype(jnp.bfloat16)


def dynamics(plan, pos, coeffs, blocks, sv, sq):
    ana, syn = zonal_tables(plan)
    smem = pl.BlockSpec(memory_space=pltpu.SMEM)
    vmem = pl.BlockSpec(memory_space=pltpu.VMEM)
    waves = (2, plan.nf * plan.levs * plan.block, plan.n_lat)
    return pl.pallas_call(
        functools.partial(dynamics_kernel, plan, len(blocks)),
        out_shape=(
            jax.ShapeDtypeStruct(blocks[0].shape, jnp.float32),
            jax.ShapeDtypeStruct((plan.lon_dev, plan.feats, plan.lat_dev), jnp.bfloat16),
        ),
        in_specs=[smem, smem] + [vmem] * (len(blocks) + 5),
        out_specs=(vmem, vmem),
        scratch_shapes=[
            pltpu.VMEM((plan.lats, plan.nf, plan.levs, plan.rows, plan.lat_dev), jnp.float32),
            pltpu.VMEM(waves, jnp.bfloat16),
            pltpu.VMEM(waves, jnp.bfloat16),
            pltpu.VMEM((plan.lats, plan.levs, plan.rows, plan.lat_dev), jnp.float32),
            pltpu.VMEM((plan.lon_dev, plan.feats, plan.lat_dev), jnp.float32),
        ],
        compiler_params=pltpu.CompilerParams(vmem_limit_bytes=32 * 1024 * 1024),
        name="dynamics",
    )(pos, coeffs, *blocks, jnp.asarray(ana), jnp.asarray(syn), jnp.asarray(meridional_tables(plan)), sv, sq)


def half_silu(half):
    return (half + half * jnp.tanh(half)).astype(jnp.bfloat16)


def network_kernel(plan, blocks, group, *refs):
    block_refs = refs[:blocks]
    state_ref, w1_ref, mid_ref, wo_ref = refs[blocks : blocks + 4]
    out_ref, tile_ref = refs[blocks + 4 :]
    mids = [(0.5 * mid_ref[n]).astype(jnp.bfloat16) for n in range(2)]
    for first in range(0, plan.lon_dev, group):
        lons = range(first, min(first + group, plan.lon_dev))
        inputs = jnp.concatenate(
            [
                jnp.concatenate([ref[lon].astype(jnp.float32) for ref in block_refs], axis=0).astype(jnp.bfloat16)
                for lon in lons
            ],
            axis=1,
        )
        hidden = half_silu(mm(w1_ref[...], inputs))
        hidden = half_silu(mm(mids[0], hidden))
        hidden = half_silu(mm(mids[1], hidden))
        output = mm(wo_ref[...], hidden).astype(jnp.bfloat16).astype(jnp.float32)
        for n, lon in enumerate(lons):
            tile_ref[lon] = output[:, n * plan.lat_dev : (n + 1) * plan.lat_dev]
    for f in range(plan.nf):
        for l in range(plan.levs):
            out_ref[f, l] = state_ref[f, l] + tile_ref[:, f * plan.levs + l, :]


def network(plan, state, blocks, w1, mid, wo):
    vmem = pl.BlockSpec(memory_space=pltpu.VMEM)
    group = max(1, 768 // plan.lat_dev)
    return pl.pallas_call(
        functools.partial(network_kernel, plan, len(blocks), group),
        out_shape=jax.ShapeDtypeStruct(state.shape, jnp.float32),
        in_specs=[vmem] * (len(blocks) + 4),
        out_specs=vmem,
        scratch_shapes=[pltpu.VMEM((plan.lon_dev, plan.feats, plan.lat_dev), jnp.float32)],
        compiler_params=pltpu.CompilerParams(vmem_limit_bytes=32 * 1024 * 1024),
        name="network",
    )(*blocks, state, w1, mid, wo)


def swap(value, axes, sizes, mask):
    count = int(np.prod(sizes))
    return lax.ppermute(value, axes, [(i, i ^ mask) for i in range(count)])


def gathering(plan, fields, spectral_coeffs, mlp_in, mlp_mid, mlp_out):
    pos = jnp.stack([lax.axis_index("lon"), lax.axis_index("lat"), lax.axis_index("lev")]).astype(jnp.int32)
    plane = ("lon", "lat")
    sizes = (plan.lons, plan.lats)
    blocks = [None] * (plan.lons * plan.lats)
    outer = [(lon, lat) for lat in range(0, plan.lats, 2) for lon in range(plan.lons)]
    for lon, lat in outer:
        mask = lon * plan.lats + lat
        blocks[lat * plan.lons + lon] = swap(fields, plane, sizes, mask) if mask else fields
    if plan.lats > 1:
        for lon, lat in outer:
            blocks[(lat ^ 1) * plan.lons + lon] = swap(blocks[lat * plan.lons + lon], plane, sizes, 1)
    sv, sq, w1, wo = prepare(plan, pos, spectral_coeffs, mlp_in, mlp_out)
    state, feats = dynamics(plan, pos, spectral_coeffs, blocks, sv, sq)
    columns = [feats]
    mask = 1
    while mask < plan.zs:
        columns = columns + [swap(part, ("lev",), (plan.zs,), mask) for part in columns]
        mask *= 2
    return network(plan, state, columns, w1, mlp_mid, wo)


def solution(mesh):
    def per_device(fields, spectral_coeffs, mlp_in, mlp_mid, mlp_out):
        plan = Plan(mesh.shape, fields.shape)
        if plan.fits():
            return gathering(plan, fields, spectral_coeffs, mlp_in, mlp_mid, mlp_out)
        return transposing(fields, spectral_coeffs, mlp_in, mlp_mid, mlp_out)

    in_specs = (P(None, "lev", "lon", "lat"), P(None, "lev"), P(), P(), P())
    out_specs = P(None, "lev", "lon", "lat")
    return jax.shard_map(
        per_device, mesh=mesh, in_specs=in_specs, out_specs=out_specs, check_vma=False
    )
```

```python
import functools

import jax
import jax.numpy as jnp
import numpy as np
from jax import lax
from jax.experimental import pallas as pl
from jax.experimental.pallas import tpu as pltpu
from jax.sharding import PartitionSpec as P


WAVES = 320
KMAX = 320
SUBSTEPS = 2


highest = lax.Precision.HIGHEST
LANES = 128
GROUP = 2048
PLANE_LIMIT = 4 * 1024 * 1024


def round_up(value, unit):
    return -(-value // unit) * unit


def forward_table(lon_ids, total_lon, waves):
    wave_ids = jnp.arange(waves, dtype=jnp.int32)
    phase = (lon_ids[:, None] * wave_ids[None, :] % total_lon).astype(jnp.float32) * (
        2.0 * jnp.pi / total_lon
    )
    return jnp.concatenate([jnp.cos(phase), -jnp.sin(phase)], axis=1) / total_lon


def inverse_table(lon_ids, total_lon, waves):
    wave_ids = jnp.arange(waves, dtype=jnp.int32)
    phase = (wave_ids[:, None] * lon_ids[None, :] % total_lon).astype(jnp.float32) * (
        2.0 * jnp.pi / total_lon
    )
    weight = jnp.where(wave_ids == 0, 1.0, 2.0).astype(jnp.float32)[:, None]
    return jnp.concatenate([weight * jnp.cos(phase), -weight * jnp.sin(phase)], axis=0)


def latitude_tables(lat_ids, total_lat, degree_ids):
    odd_rows = 2 * lat_ids[:, None] + 1
    period = 4 * total_lat
    scale = jnp.pi / (2.0 * total_lat)
    even_arg = (odd_rows * degree_ids[None, :] % period).astype(jnp.float32) * scale
    odd_arg = (odd_rows * (degree_ids[None, :] + 1) % period).astype(jnp.float32) * scale
    return (jnp.cos(even_arg), jnp.sin(odd_arg))


def latitude_forward(waves, even_tab, odd_tab):
    cols, nf, levs, lats = waves.shape
    pairs = waves.reshape(cols // 2, 2, nf, levs, lats)
    even_part = jnp.einsum("pfli,ik->pflk", pairs[:, 0], even_tab, precision=highest)
    odd_part = jnp.einsum("pfli,ik->pflk", pairs[:, 1], odd_tab, precision=highest)
    return jnp.stack([even_part, odd_part], axis=1).reshape(cols, nf, levs, even_tab.shape[1])


def latitude_inverse(spectra, even_tab, odd_tab):
    cols, nf, levs, degs = spectra.shape
    pairs = spectra.reshape(cols // 2, 2, nf, levs, degs)
    even_part = jnp.einsum("pflk,ik->pfli", pairs[:, 0], even_tab, precision=highest)
    odd_part = jnp.einsum("pflk,ik->pfli", pairs[:, 1], odd_tab, precision=highest)
    return jnp.stack([even_part, odd_part], axis=1).reshape(cols, nf, levs, even_tab.shape[0])


def operator(spectra, coeffs, col_waves, degree_ids):
    parity = col_waves % 2
    freq = (degree_ids[None, :] + parity[:, None]).astype(jnp.float32)
    wavenum = col_waves.astype(jnp.float32)[:, None]
    qvalue = ((wavenum * wavenum + freq * freq) / (KMAX * KMAX))[:, None, :]
    hyper = coeffs[0][None, :, None]
    coupling = coeffs[1][None, :, None]
    depth = coeffs[2][None, :, None]
    vort = spectra[:, 0]
    diverg = spectra[:, 1]
    temper = spectra[:, 2]
    new_vort = vort / (1.0 + hyper * qvalue * qvalue)
    new_div = (diverg + coupling * qvalue * temper) / (1.0 + coupling * depth * qvalue)
    new_temp = temper - depth * new_div
    return jnp.stack([new_vort - vort, new_div - diverg, new_temp - temper], axis=1)


def nonlinear(state):
    temper = state[2] + 0.25 * state[0] * state[1]
    return jnp.stack([state[0], state[1], temper], axis=0)


def transposing(fields, spectral_coeffs, mlp_in, mlp_mid, mlp_out):
    nf, lev_dev, lon_dev, lat_dev = fields.shape
    lon_count = lax.axis_size("lon")
    lat_count = lax.axis_size("lat")
    total_lon = lon_dev * lon_count
    total_lat = lat_dev * lat_count
    wave_cols = 2 * WAVES // lon_count
    row_count = nf * lev_dev * lat_dev
    lat_ids = lax.axis_index("lat") * lat_dev + jnp.arange(lat_dev, dtype=jnp.int32)
    col_waves = (lax.axis_index("lon") * wave_cols + jnp.arange(wave_cols, dtype=jnp.int32)) % WAVES
    weight = 2.0 / total_lat
    all_lons = jnp.arange(total_lon, dtype=jnp.int32)
    fwd_full = forward_table(all_lons, total_lon, WAVES)
    inv_full = inverse_table(all_lons, total_lon, WAVES)
    own_degrees = jnp.arange(KMAX, dtype=jnp.int32)
    full_even, full_odd = latitude_tables(lat_ids, total_lat, own_degrees)
    state = fields
    for _ in range(SUBSTEPS):
        flat = state.transpose(0, 1, 3, 2).reshape(row_count, lon_dev)
        by_row = lax.all_to_all(flat, "lon", split_axis=0, concat_axis=1, tiled=True)
        row_waves = jnp.dot(by_row, fwd_full, precision=highest)
        by_col = lax.all_to_all(row_waves, "lon", split_axis=1, concat_axis=0, tiled=True)
        waves = by_col.reshape(nf, lev_dev, lat_dev, wave_cols).transpose(3, 0, 1, 2)
        partial_spectra = latitude_forward(waves, full_even * weight, full_odd * weight)
        spectra = lax.psum(partial_spectra, "lat")
        change = operator(spectra, spectral_coeffs, col_waves, own_degrees)
        back = latitude_inverse(change, full_even, full_odd)
        flat_back = back.transpose(1, 2, 3, 0).reshape(row_count, wave_cols)
        full_waves = lax.all_to_all(flat_back, "lon", split_axis=0, concat_axis=1, tiled=True)
        row_grid = jnp.dot(full_waves, inv_full, precision=highest)
        own_grid = lax.all_to_all(row_grid, "lon", split_axis=1, concat_axis=0, tiled=True)
        increment = own_grid.reshape(nf, lev_dev, lat_dev, lon_dev).transpose(0, 1, 3, 2)
        state = nonlinear(state + increment)
    features = state.astype(jnp.bfloat16).reshape(nf, lev_dev, lon_dev * lat_dev)
    columns = lax.all_to_all(features, "lev", split_axis=2, concat_axis=1, tiled=True)
    levels = columns.shape[1]
    inputs = columns.reshape(nf * levels, columns.shape[2])
    hidden = jax.nn.silu(jnp.dot(mlp_in, inputs, preferred_element_type=jnp.float32)).astype(
        jnp.bfloat16
    )
    hidden = jax.nn.silu(jnp.dot(mlp_mid[0], hidden, preferred_element_type=jnp.float32)).astype(
        jnp.bfloat16
    )
    hidden = jax.nn.silu(jnp.dot(mlp_mid[1], hidden, preferred_element_type=jnp.float32)).astype(
        jnp.bfloat16
    )
    output = jnp.dot(mlp_out, hidden, preferred_element_type=jnp.float32).astype(jnp.bfloat16)
    output = output.reshape(nf, levels, columns.shape[2])
    returned = lax.all_to_all(output, "lev", split_axis=1, concat_axis=2, tiled=True)
    return state + returned.astype(jnp.float32).reshape(state.shape)


class Plan:
    def __init__(self, mesh_shape, local):
        self.nf, self.levs, self.lon_dev, self.lat_dev = local
        self.lons = mesh_shape["lon"]
        self.lats = mesh_shape["lat"]
        self.zs = mesh_shape["lev"]
        self.n_lon = self.lons * self.lon_dev
        self.n_lat = self.lats * self.lat_dev
        self.jpad = round_up(self.lon_dev, 16)
        self.rows = self.lons * self.jpad
        classes = min(self.n_lon // 2 + 1, WAVES)
        self.half = round_up((classes + 1) // 2, 16)
        self.block = 2 * self.half
        self.modes = 2 * self.block
        self.degs = round_up(-(-KMAX // 2), 16)
        self.side = self.lats // 2
        self.feats = round_up(self.nf * self.levs, 8)
        self.chunks = [(0, self.lon_dev)]

    def fits(self):
        plane = self.nf * self.levs * self.n_lon * self.n_lat * 4
        power_of_two = all(n & (n - 1) == 0 for n in (self.lons, self.lats, self.zs))
        return (
            SUBSTEPS == 2
            and self.nf == 3
            and power_of_two
            and plane <= PLANE_LIMIT
            and self.n_lon % 2 == 0
            and self.lats % 2 == 0
            and self.lat_dev == LANES
            and KMAX < self.n_lat
        )


def split_np(table):
    high = table.astype(np.float32).astype(jnp.bfloat16)
    low = (table - high.astype(np.float64)).astype(jnp.bfloat16)
    return high, low


def zonal_tables(plan):
    lon = np.arange(plan.n_lon)
    pos = (lon // plan.lon_dev) * plan.jpad + lon % plan.lon_dev
    scale = 2.0 / (plan.n_lon * plan.n_lat)
    ana = np.zeros((plan.modes, plan.rows))
    syn = np.zeros((plan.rows, plan.modes))
    classes = min(plan.n_lon // 2 + 1, WAVES)
    for rho in range(classes):
        phase = 2.0 * np.pi * ((rho * lon) % plan.n_lon) / plan.n_lon
        cos_row = (rho % 2) * plan.block + rho // 2
        ana[cos_row, pos] = scale * np.cos(phase)
        syn[pos, cos_row] = np.cos(phase)
        if rho > 0 and 2 * rho != plan.n_lon:
            ana[cos_row + plan.half, pos] = -scale * np.sin(phase)
            syn[pos, cos_row + plan.half] = -np.sin(phase)
    ana_h, ana_l = split_np(ana)
    syn_h, syn_l = split_np(syn)
    return (
        np.concatenate([ana_h, ana_l, ana_h], axis=1),
        np.concatenate([syn_h, syn_l, syn_h], axis=1),
    )


def meridional_tables(plan):
    lat = np.arange(plan.n_lat // 2)[None, :]
    deg = np.arange(KMAX)[:, None]
    period = 4 * plan.n_lat
    scale = np.pi / (2.0 * plan.n_lat)
    even = np.cos(((2 * lat + 1) * deg % period) * scale)
    odd = np.sin(((2 * lat + 1) * (deg + 1) % period) * scale)
    out = np.zeros((2, 2, 2, plan.degs, plan.n_lat // 2), dtype=jnp.bfloat16)
    for parity, table in enumerate((even, odd)):
        for kind in range(2):
            for part, value in enumerate(split_np(table[kind::2])):
                out[parity, kind, part, : value.shape[0]] = value
    return out


def split(value):
    high = value.astype(jnp.bfloat16)
    low = (value - high.astype(jnp.float32)).astype(jnp.bfloat16)
    return high, low


def mm(left, right):
    return lax.dot_general(
        left, right, (((1,), (0,)), ((), ())), preferred_element_type=jnp.float32
    )


def mm_l(left, right):
    return lax.dot_general(
        left, right, (((0,), (0,)), ((), ())), preferred_element_type=jnp.float32
    )


def mm_t(left, right):
    return lax.dot_general(
        left, right, (((1,), (1,)), ((), ())), preferred_element_type=jnp.float32
    )


def prepare_kernel(plan, coef_hbm, *refs):
    sources, refs = refs[:3], refs[3:]
    sv_ref, sq_ref, gb_ref = refs[:3]
    targets, (coef_ref, sems) = refs[3:6], refs[6:]
    first = pltpu.make_async_copy(coef_hbm, coef_ref, sems.at[3])
    first.start()
    copies = [pltpu.make_async_copy(source, target, sems.at[n]) for n, (source, target) in enumerate(zip(sources, targets))]
    for copy in copies:
        copy.start()
    first.wait()
    for lev in range(plan.levs):
        gb_ref[lev] = jnp.full(gb_ref.shape[1:], coef_ref[lev, 2], jnp.float32)
    row = lax.broadcasted_iota(jnp.int32, (plan.half, plan.degs), 0)
    lane = lax.broadcasted_iota(jnp.int32, (plan.half, plan.degs), 1)
    inv_k2 = 1.0 / (KMAX * KMAX)
    turns = -(-WAVES // plan.n_lon)
    for parity in range(2):
        rho = 2 * row + parity
        terms = []
        for turn in range(turns):
            wave = rho + plan.n_lon * turn
            terms.append((wave, (wave < WAVES) & (2 * rho <= plan.n_lon)))
            wave = plan.n_lon * (turn + 1) - rho
            terms.append((wave, (wave < WAVES) & (rho > 0) & (2 * rho < plan.n_lon)))
        terms = [
            (wave.astype(jnp.float32), jnp.where(valid, jnp.where(wave == 0, 1.0, 2.0), 0.0)) for wave, valid in terms
        ]
        for kind in range(2):
            freq = (2 * lane + kind + parity).astype(jnp.float32)
            freq2 = freq * freq
            sums = [[jnp.zeros((plan.half, plan.degs), jnp.float32) for _ in range(2)] for _ in range(plan.levs)]
            for wave, weight in terms:
                q = (wave * wave + freq2) * inv_k2
                for lev in range(plan.levs):
                    nu, ga, gb = (coef_ref[lev, i] for i in range(3))
                    hyper = nu * q * q
                    wave_q = ga * q
                    sums[lev][0] -= weight * (hyper / (1.0 + hyper))
                    sums[lev][1] += weight * (wave_q / (1.0 + gb * wave_q))
            for lev in range(plan.levs):
                sv_ref[lev, parity, kind] = sums[lev][0]
                sq_ref[lev, parity, kind] = sums[lev][1]
    for copy in copies:
        copy.wait()


def prepare(plan, coeffs):
    table = jax.ShapeDtypeStruct((plan.levs, 2, 2, plan.half, plan.degs), jnp.float32)
    vmem = pl.BlockSpec(memory_space=pltpu.VMEM)
    tables = [jnp.asarray(t) for t in (*zonal_tables(plan), meridional_tables(plan))]
    out = pl.pallas_call(
        functools.partial(prepare_kernel, plan),
        out_shape=(
            table,
            table,
            jax.ShapeDtypeStruct((plan.levs, 8, LANES), jnp.float32),
            *(jax.ShapeDtypeStruct(t.shape, t.dtype) for t in tables),
        ),
        in_specs=[pl.BlockSpec(memory_space=pltpu.HBM)] * (1 + len(tables)),
        out_specs=(vmem,) * (3 + len(tables)),
        scratch_shapes=[pltpu.SMEM(coeffs.shape, jnp.float32), pltpu.SemaphoreType.DMA((1 + len(tables),))],
        compiler_params=pltpu.CompilerParams(vmem_limit_bytes=16 * 1024 * 1024),
        name="prepare",
    )(*[pltpu.with_memory_space_constraint(t, pltpu.HBM) for t in (coeffs, *tables)])
    return out[:3], out[3:]


def weights_kernel(plan, win_ref, mid_ref, wout_ref, w1_ref, half_ref, wo_ref):
    half_ref[...] = (0.5 * mid_ref[...].astype(jnp.float32)).astype(jnp.bfloat16)
    own_z = lax.axis_index("lev")
    total = plan.zs * plan.levs
    nin = plan.nf * total

    def feature_of(slot, count):
        block = slot // count
        inner = slot % count
        field = inner // plan.levs
        level = (own_z ^ block) * plan.levs + inner % plan.levs
        return jnp.where(inner < plan.nf * plan.levs, field * total + level, -1)

    count = plan.nf * plan.levs
    wide = plan.zs * count
    source = lax.broadcasted_iota(jnp.int32, (nin, wide), 0)
    slot = lax.broadcasted_iota(jnp.int32, (nin, wide), 1)
    pick = (source == feature_of(slot, count)).astype(jnp.float32).astype(jnp.bfloat16)
    w1_ref[...] = (0.5 * mm_l(win_ref[...], pick)).astype(jnp.bfloat16)
    slot = lax.broadcasted_iota(jnp.int32, (plan.feats, nin), 0)
    source = lax.broadcasted_iota(jnp.int32, (plan.feats, nin), 1)
    pick = (source == feature_of(slot, plan.feats)).astype(jnp.float32).astype(jnp.bfloat16)
    wo_ref[...] = mm(pick, wout_ref[...]).astype(jnp.bfloat16)


def order_weights(plan, mlp_in, mlp_mid, mlp_out):
    units = mlp_in.shape[1]
    vmem = pl.BlockSpec(memory_space=pltpu.VMEM)
    return pl.pallas_call(
        functools.partial(weights_kernel, plan),
        out_shape=(
            jax.ShapeDtypeStruct((units, plan.zs * plan.nf * plan.levs), jnp.bfloat16),
            jax.ShapeDtypeStruct(mlp_mid.shape, jnp.bfloat16),
            jax.ShapeDtypeStruct((plan.feats, units), jnp.bfloat16),
        ),
        in_specs=[vmem] * 3,
        out_specs=(vmem,) * 3,
        compiler_params=pltpu.CompilerParams(vmem_limit_bytes=16 * 1024 * 1024),
        name="order_weights",
    )(mlp_in, mlp_mid, mlp_out)


def dynamics_kernel(plan, blocks, *refs):
    block_refs = refs[:blocks]
    ana_ref, syn_ref, mer_ref, sv_ref, sq_ref, gb_ref = refs[blocks : 6 + blocks]
    state_ref, feat_refs = refs[6 + blocks], refs[7 + blocks : 7 + blocks + len(plan.chunks)]
    grid_ref, wh_ref, wl_ref, prod_ref = refs[7 + blocks + len(plan.chunks) :]
    own_lon, own_lat = lax.axis_index("lon"), lax.axis_index("lat")
    nf, levs, lats = plan.nf, plan.levs, plan.lats
    block, half = plan.block, plan.half
    if plan.jpad != plan.lon_dev:
        tail = (plan.lon_dev // 8) * 8
        for lon in range(plan.lons):
            start = lon * plan.jpad + tail
            stop = (lon + 1) * plan.jpad
            zeros = jnp.zeros((stop - start, plan.lat_dev), jnp.float32)
            for side in range(2):
                for lat in range(plan.side):
                    for f in range(nf):
                        for l in range(levs):
                            grid_ref[side, lat, f, l, start:stop, :] = zeros

    def place(lat):
        south = lat >= plan.side
        return jnp.where(south, 1, 0), jnp.where(south, lats - 1 - lat, lat)

    def mirror(value, side):
        lane = lax.broadcasted_iota(jnp.int32, value.shape, 1)
        lane = jnp.where(side == 1, plan.lat_dev - 1 - lane, lane)
        return jnp.take_along_axis(value, lane, axis=1, mode="promise_in_bounds")

    for s in range(blocks):
        lon = own_lon ^ (s % plan.lons)
        side, lat = place(own_lat ^ (s // plan.lons))
        row = pl.multiple_of(lon * plan.jpad, 8)
        for f in range(nf):
            for l in range(levs):
                value = block_refs[s][f, :, l, :]
                grid_ref[side, lat, f, l, pl.ds(row, plan.lon_dev), :] = mirror(value, side)

    def whole(ref, side, *index):
        return jnp.concatenate([ref[(side, lat, *index)] for lat in range(plan.side)], axis=1)

    def analyse(values):
        middle = plan.n_lat // 2
        for n, (north, south) in enumerate(values):
            high, low = split(jnp.concatenate([north + south, north - south], axis=1))
            waves = mm(ana_ref[...], jnp.concatenate([high, high, low], axis=0))
            high, low = split(waves)
            for parity in range(2):
                rows = slice(parity * block, (parity + 1) * block)
                wh_ref[parity, n * block : (n + 1) * block, :] = high[rows]
                wl_ref[parity, n * block : (n + 1) * block, :] = low[rows]
        size = len(values) * block
        out = []
        for parity in range(2):
            kinds = []
            for kind in range(2):
                lanes = slice(kind * middle, (kind + 1) * middle)
                high, low = wh_ref[parity, :size, lanes], wl_ref[parity, :size, lanes]
                thigh, tlow = mer_ref[parity, kind, 0], mer_ref[parity, kind, 1]
                kinds.append(mm_t(high, thigh) + mm_t(low, thigh) + mm_t(high, tlow))
            out.append(kinds)
        return out

    def synthesise(spectra, rows, table):
        parts = []
        for parity in range(2):
            kinds = []
            for kind in range(2):
                high, low = split(spectra[parity][kind])
                thigh, tlow = table(parity, kind)
                kinds.append(mm(high, thigh) + mm(low, thigh) + mm(high, tlow))
            parts.append(jnp.concatenate(kinds, axis=1))
        count = spectra[0][0].shape[0] // block
        width = parts[0].shape[1] // 2
        out = []
        for n in range(count):
            both = jnp.concatenate([part[n * block : (n + 1) * block] for part in parts], axis=0)
            high, low = split(both)
            grid = mm(rows, jnp.concatenate([high, high, low], axis=0))
            out.append((grid[:, :width], grid[:, width:]))
        return out

    def at(spectrum, f, l):
        n = f * levs + l
        return spectrum[n * block : (n + 1) * block]

    pairs = [(parity, kind) for parity in range(2) for kind in range(2)]
    lane = lax.broadcasted_iota(jnp.int32, (block, plan.degs), 1)
    cls = lax.broadcasted_iota(jnp.int32, (block, plan.degs), 0) % half
    norms, counts = {}, {}
    for parity in range(2):
        rho = 2 * cls + parity
        alone = (rho == 0) | (2 * rho == plan.n_lon)
        norm = jnp.where(alone, 1.0, 0.5)
        weight = jnp.zeros((block, plan.degs), jnp.float32)
        for turn in range(-(-WAVES // plan.n_lon)):
            wave = rho + plan.n_lon * turn
            weight += jnp.where(wave < WAVES, jnp.where(wave == 0, 1.0, 2.0), 0.0)
            wave = plan.n_lon * (turn + 1) - rho
            weight += jnp.where((wave < WAVES) & (rho > 0) & (2 * rho < plan.n_lon), 2.0, 0.0)
        for kind in range(2):
            counts[parity, kind] = weight
            norms[parity, kind] = norm * jnp.where(lane == 0, 2.0, 1.0) if parity == kind == 0 else norm

    def changes(spectra):
        out = {}
        for pair in pairs:
            per = [[None] * levs for _ in range(nf)]
            for l in range(levs):
                sv = jnp.concatenate([sv_ref[(l, *pair)]] * 2, axis=0)
                sq = jnp.concatenate([sq_ref[(l, *pair)]] * 2, axis=0)
                gb = gb_ref[l, 0:1, 0:1]
                vort, diverg, temper = (spectra[pair][f][l] for f in range(3))
                per[0][l] = sv * vort
                per[1][l] = sq * (temper - gb * diverg)
                per[2][l] = -gb * (counts[pair] * diverg + per[1][l])
            out[pair] = per
        return out

    def stack(nested, fields):
        return [
            [
                jnp.concatenate([nested[parity, kind][f][l] for f in fields for l in range(levs)], axis=0)
                for kind in range(2)
            ]
            for parity in range(2)
        ]

    flat = analyse([tuple(whole(grid_ref, side, f, l) for side in range(2)) for f in range(nf) for l in range(levs)])
    spectra = {
        (parity, kind): [[at(flat[parity][kind], f, l) for l in range(levs)] for f in range(nf)]
        for parity, kind in pairs
    }
    first = changes(spectra)
    grown = synthesise(
        stack(first, (0, 1)), syn_ref[...], lambda parity, kind: (mer_ref[parity, kind, 0], mer_ref[parity, kind, 1])
    )
    products = []
    for l in range(levs):
        (vsym, vanti), (dsym, danti) = grown[l], grown[levs + l]
        sides = []
        for side in range(2):
            vort = whole(grid_ref, side, 0, l) + (vsym - vanti if side else vsym + vanti)
            diverg = whole(grid_ref, side, 1, l) + (dsym - danti if side else dsym + danti)
            product = 0.25 * vort * diverg
            for lat in range(plan.side):
                prod_ref[side, lat, l] = product[:, lat * plan.lat_dev : (lat + 1) * plan.lat_dev]
            sides.append(product)
        products.append(tuple(sides))
    extra = analyse(products)
    updated = {}
    for pair in pairs:
        per = [[spectra[pair][f][l] + norms[pair] * first[pair][f][l] for l in range(levs)] for f in range(nf)]
        per[2] = [per[2][l] + at(extra[pair[0]][pair[1]], 0, l) for l in range(levs)]
        updated[pair] = per
    second = changes(updated)
    both = {
        pair: [[first[pair][f][l] + second[pair][f][l] for l in range(levs)] for f in range(nf)] for pair in pairs
    }
    side, lat = place(own_lat)
    own_start = pl.multiple_of(lat * plan.lat_dev, LANES)
    own_row = pl.multiple_of(own_lon * plan.jpad, 8)
    own = synthesise(
        stack(both, range(nf)),
        syn_ref[pl.ds(own_row, plan.jpad), :],
        lambda parity, kind: tuple(mer_ref[parity, kind, part, :, pl.ds(own_start, plan.lat_dev)] for part in range(2)),
    )
    sign = jnp.where(side == 1, -1.0, 1.0)
    for l in range(levs):
        vort, diverg, temper = (
            grid_ref[side, lat, f, l, pl.ds(own_row, plan.jpad), :]
            + (own[f * levs + l][0] + sign * own[f * levs + l][1])
            for f in range(3)
        )
        temper = temper + prod_ref[side, lat, l, pl.ds(own_row, plan.jpad), :] + 0.25 * vort * diverg
        for f, value in enumerate((vort, diverg, temper)):
            value = mirror(value, side)
            state_ref[f, l] = value[: plan.lon_dev]
            rounded = value.astype(jnp.bfloat16)
            for (start, _), ref in zip(plan.chunks, feat_refs):
                ref[f * levs + l] = rounded[start : start + ref.shape[1]]


def dynamics(plan, blocks, tables, sums):
    vmem = pl.BlockSpec(memory_space=pltpu.VMEM)
    waves = (2, plan.nf * plan.levs * plan.block, plan.n_lat)
    return pl.pallas_call(
        functools.partial(dynamics_kernel, plan, len(blocks)),
        out_shape=(
            jax.ShapeDtypeStruct((plan.nf, plan.levs, plan.lon_dev, plan.lat_dev), jnp.float32),
            *(
                jax.ShapeDtypeStruct((plan.nf * plan.levs, round_up(stop - start, 16), plan.lat_dev), jnp.bfloat16)
                for start, stop in plan.chunks
            ),
        ),
        in_specs=[vmem] * (len(blocks) + 6),
        out_specs=(vmem,) * (1 + len(plan.chunks)),
        scratch_shapes=[
            pltpu.VMEM((2, plan.side, plan.nf, plan.levs, plan.rows, plan.lat_dev), jnp.float32),
            pltpu.VMEM(waves, jnp.bfloat16),
            pltpu.VMEM(waves, jnp.bfloat16),
            pltpu.VMEM((2, plan.side, plan.levs, plan.rows, plan.lat_dev), jnp.float32),
        ],
        compiler_params=pltpu.CompilerParams(vmem_limit_bytes=32 * 1024 * 1024),
        name="dynamics",
    )(*blocks, *tables, *sums)


def silu_of_half(half):
    return (half + half * jnp.tanh(half)).astype(jnp.bfloat16)


def network_kernel(plan, chunk, done, blocks, *refs):
    start, stop = plan.chunks[chunk]
    block_refs = refs[:blocks]
    w1_ref, mid_ref, wo_ref = refs[blocks : blocks + 3]
    refs = refs[blocks + 3 :]
    last = chunk == len(plan.chunks) - 1
    if last:
        state_ref, tiles, out_ref = refs[0], list(refs[1 : 1 + done]), refs[1 + done]
        wide_ref, tile_ref, sum_ref, sem = refs[2 + done :]
        tiles.append(tile_ref)
    else:
        tile_ref, wide_ref = refs
    copies = []

    def finish(number):
        begin, end = plan.chunks[number]
        for f in range(plan.nf):
            for l in range(plan.levs):
                row = f * plan.levs + l
                sum_ref[f, begin:end, l, :] = state_ref[f, l, begin:end, :] + tiles[number][: end - begin, row, :]
            part = (f, pl.ds(begin, end - begin))
            copy = pltpu.make_async_copy(sum_ref.at[part], out_ref.at[part], sem.at[number, f])
            copy.start()
            copies.append(copy)

    if last:
        for number in range(done):
            finish(number)
    stride = block_refs[0].shape[1]
    rows = plan.nf * plan.levs * stride
    for s, ref in enumerate(block_refs):
        wide_ref[s * rows : (s + 1) * rows, :] = ref[...].astype(jnp.float32).reshape(rows, plan.lat_dev)
    count = blocks * plan.nf * plan.levs
    group = max(1, GROUP // plan.lat_dev)
    for first in range(0, stop - start, group):
        lons = range(first, min(first + group, stop - start))
        inputs = jnp.concatenate(
            [wide_ref[pl.ds(lon, count, stride=stride), :].astype(jnp.bfloat16) for lon in lons],
            axis=1,
        )
        hidden = silu_of_half(mm(w1_ref[...], inputs))
        hidden = silu_of_half(mm(mid_ref[0], hidden))
        hidden = silu_of_half(mm(mid_ref[1], hidden))
        output = mm(wo_ref[...], hidden).astype(jnp.bfloat16).astype(jnp.float32)
        for n, lon in enumerate(lons):
            tile_ref[lon] = output[:, n * plan.lat_dev : (n + 1) * plan.lat_dev]
    if last:
        finish(chunk)
        for copy in copies:
            copy.wait()


def network(plan, chunk, blocks, weights, state, tiles):
    vmem = pl.BlockSpec(memory_space=pltpu.VMEM)
    start, stop = plan.chunks[chunk]
    last = chunk == len(plan.chunks) - 1
    tile = (stop - start, plan.feats, plan.lat_dev)
    wide = (len(blocks) * plan.nf * plan.levs * blocks[0].shape[1], plan.lat_dev)
    out = (plan.nf, plan.lon_dev, plan.levs, plan.lat_dev)
    scratch = [pltpu.VMEM(wide, jnp.float32)]
    if last:
        scratch += [
            pltpu.VMEM(tile, jnp.float32),
            pltpu.VMEM(out, jnp.float32),
            pltpu.SemaphoreType.DMA((len(plan.chunks), plan.nf)),
        ]
    extra = (state, *tiles) if last else ()
    return pl.pallas_call(
        functools.partial(network_kernel, plan, chunk, len(tiles), len(blocks)),
        out_shape=jax.ShapeDtypeStruct(out if last else tile, jnp.float32),
        in_specs=[vmem] * (len(blocks) + 3 + len(extra)),
        out_specs=pl.BlockSpec(memory_space=pltpu.HBM) if last else vmem,
        scratch_shapes=scratch,
        compiler_params=pltpu.CompilerParams(vmem_limit_bytes=24 * 1024 * 1024),
    )(*blocks, *weights, *extra)


def swap(value, axes, sizes, mask):
    count = int(np.prod(sizes))
    return lax.ppermute(value, axes, [(i, i ^ mask) for i in range(count)])


def gathering(plan, fields, spectral_coeffs, mlp_in, mlp_mid, mlp_out):
    fields = fields.transpose(0, 2, 1, 3)
    plane = ("lon", "lat")
    sizes = (plan.lons, plan.lats)
    blocks = [None] * (plan.lons * plan.lats)
    outer = [(lon, lat) for lat in range(0, plan.lats, 2) for lon in range(plan.lons)]
    for lon, lat in outer:
        mask = lon * plan.lats + lat
        blocks[lat * plan.lons + lon] = swap(fields, plane, sizes, mask) if mask else fields
    if plan.lats > 1:
        for lon, lat in outer:
            blocks[(lat ^ 1) * plan.lons + lon] = swap(blocks[lat * plan.lons + lon], plane, sizes, 1)
    sums, tables = prepare(plan, spectral_coeffs.T)
    weights = order_weights(plan, mlp_in.T, mlp_mid, mlp_out)
    state, *feats = dynamics(plan, blocks, tables, sums)
    columns = []
    for own in feats:
        parts = [own]
        for mask in range(1, plan.zs):
            parts.append(swap(own, ("lev",), (plan.zs,), mask))
        columns.append(parts)
    tiles = []
    for chunk, parts in enumerate(columns):
        tiles.append(network(plan, chunk, parts, weights, state, tiles))
    return tiles[-1].transpose(0, 2, 1, 3)


def solution(mesh):
    in_specs = (P(None, "lev", "lon", "lat"), P(None, "lev"), P(), P(), P())
    out_specs = P(None, "lev", "lon", "lat")

    def per_device(fields, spectral_coeffs, mlp_in, mlp_mid, mlp_out):
        plan = Plan(mesh.shape, fields.shape)
        if plan.fits():
            return gathering(plan, fields, spectral_coeffs, mlp_in, mlp_mid, mlp_out)
        return transposing(fields, spectral_coeffs, mlp_in, mlp_mid, mlp_out)

    def step(fields, *rest):
        return jax.shard_map(
            per_device, mesh=mesh, in_specs=in_specs, out_specs=out_specs, check_vma=False
        )(fields, *rest)

    return step
```

```python
import functools

import jax
import jax.numpy as jnp
import numpy as np
from jax import lax
from jax.experimental import pallas as pl
from jax.experimental.pallas import tpu as pltpu
from jax.sharding import PartitionSpec as P


WAVES = 320
KMAX = 320
SUBSTEPS = 2


highest = lax.Precision.HIGHEST
LANES = 128
GROUP = 2048
PLANE_LIMIT = 4 * 1024 * 1024


def round_up(value, unit):
    return -(-value // unit) * unit


def forward_table(lon_ids, total_lon, waves):
    wave_ids = jnp.arange(waves, dtype=jnp.int32)
    phase = (lon_ids[:, None] * wave_ids[None, :] % total_lon).astype(jnp.float32) * (
        2.0 * jnp.pi / total_lon
    )
    return jnp.concatenate([jnp.cos(phase), -jnp.sin(phase)], axis=1) / total_lon


def inverse_table(lon_ids, total_lon, waves):
    wave_ids = jnp.arange(waves, dtype=jnp.int32)
    phase = (wave_ids[:, None] * lon_ids[None, :] % total_lon).astype(jnp.float32) * (
        2.0 * jnp.pi / total_lon
    )
    weight = jnp.where(wave_ids == 0, 1.0, 2.0).astype(jnp.float32)[:, None]
    return jnp.concatenate([weight * jnp.cos(phase), -weight * jnp.sin(phase)], axis=0)


def latitude_tables(lat_ids, total_lat, degree_ids):
    odd_rows = 2 * lat_ids[:, None] + 1
    period = 4 * total_lat
    scale = jnp.pi / (2.0 * total_lat)
    even_arg = (odd_rows * degree_ids[None, :] % period).astype(jnp.float32) * scale
    odd_arg = (odd_rows * (degree_ids[None, :] + 1) % period).astype(jnp.float32) * scale
    return (jnp.cos(even_arg), jnp.sin(odd_arg))


def latitude_forward(waves, even_tab, odd_tab):
    cols, nf, levs, lats = waves.shape
    pairs = waves.reshape(cols // 2, 2, nf, levs, lats)
    even_part = jnp.einsum("pfli,ik->pflk", pairs[:, 0], even_tab, precision=highest)
    odd_part = jnp.einsum("pfli,ik->pflk", pairs[:, 1], odd_tab, precision=highest)
    return jnp.stack([even_part, odd_part], axis=1).reshape(cols, nf, levs, even_tab.shape[1])


def latitude_inverse(spectra, even_tab, odd_tab):
    cols, nf, levs, degs = spectra.shape
    pairs = spectra.reshape(cols // 2, 2, nf, levs, degs)
    even_part = jnp.einsum("pflk,ik->pfli", pairs[:, 0], even_tab, precision=highest)
    odd_part = jnp.einsum("pflk,ik->pfli", pairs[:, 1], odd_tab, precision=highest)
    return jnp.stack([even_part, odd_part], axis=1).reshape(cols, nf, levs, even_tab.shape[0])


def operator(spectra, coeffs, col_waves, degree_ids):
    parity = col_waves % 2
    freq = (degree_ids[None, :] + parity[:, None]).astype(jnp.float32)
    wavenum = col_waves.astype(jnp.float32)[:, None]
    qvalue = ((wavenum * wavenum + freq * freq) / (KMAX * KMAX))[:, None, :]
    hyper = coeffs[0][None, :, None]
    coupling = coeffs[1][None, :, None]
    depth = coeffs[2][None, :, None]
    vort = spectra[:, 0]
    diverg = spectra[:, 1]
    temper = spectra[:, 2]
    new_vort = vort / (1.0 + hyper * qvalue * qvalue)
    new_div = (diverg + coupling * qvalue * temper) / (1.0 + coupling * depth * qvalue)
    new_temp = temper - depth * new_div
    return jnp.stack([new_vort - vort, new_div - diverg, new_temp - temper], axis=1)


def nonlinear(state):
    temper = state[2] + 0.25 * state[0] * state[1]
    return jnp.stack([state[0], state[1], temper], axis=0)


def transposing(fields, spectral_coeffs, mlp_in, mlp_mid, mlp_out):
    nf, lev_dev, lon_dev, lat_dev = fields.shape
    lon_count = lax.axis_size("lon")
    lat_count = lax.axis_size("lat")
    total_lon = lon_dev * lon_count
    total_lat = lat_dev * lat_count
    wave_cols = 2 * WAVES // lon_count
    row_count = nf * lev_dev * lat_dev
    lat_ids = lax.axis_index("lat") * lat_dev + jnp.arange(lat_dev, dtype=jnp.int32)
    col_waves = (lax.axis_index("lon") * wave_cols + jnp.arange(wave_cols, dtype=jnp.int32)) % WAVES
    weight = 2.0 / total_lat
    all_lons = jnp.arange(total_lon, dtype=jnp.int32)
    fwd_full = forward_table(all_lons, total_lon, WAVES)
    inv_full = inverse_table(all_lons, total_lon, WAVES)
    own_degrees = jnp.arange(KMAX, dtype=jnp.int32)
    full_even, full_odd = latitude_tables(lat_ids, total_lat, own_degrees)
    state = fields
    for _ in range(SUBSTEPS):
        flat = state.transpose(0, 1, 3, 2).reshape(row_count, lon_dev)
        by_row = lax.all_to_all(flat, "lon", split_axis=0, concat_axis=1, tiled=True)
        row_waves = jnp.dot(by_row, fwd_full, precision=highest)
        by_col = lax.all_to_all(row_waves, "lon", split_axis=1, concat_axis=0, tiled=True)
        waves = by_col.reshape(nf, lev_dev, lat_dev, wave_cols).transpose(3, 0, 1, 2)
        partial_spectra = latitude_forward(waves, full_even * weight, full_odd * weight)
        spectra = lax.psum(partial_spectra, "lat")
        change = operator(spectra, spectral_coeffs, col_waves, own_degrees)
        back = latitude_inverse(change, full_even, full_odd)
        flat_back = back.transpose(1, 2, 3, 0).reshape(row_count, wave_cols)
        full_waves = lax.all_to_all(flat_back, "lon", split_axis=0, concat_axis=1, tiled=True)
        row_grid = jnp.dot(full_waves, inv_full, precision=highest)
        own_grid = lax.all_to_all(row_grid, "lon", split_axis=1, concat_axis=0, tiled=True)
        increment = own_grid.reshape(nf, lev_dev, lat_dev, lon_dev).transpose(0, 1, 3, 2)
        state = nonlinear(state + increment)
    features = state.astype(jnp.bfloat16).reshape(nf, lev_dev, lon_dev * lat_dev)
    columns = lax.all_to_all(features, "lev", split_axis=2, concat_axis=1, tiled=True)
    levels = columns.shape[1]
    inputs = columns.reshape(nf * levels, columns.shape[2])
    hidden = jax.nn.silu(jnp.dot(mlp_in, inputs, preferred_element_type=jnp.float32)).astype(
        jnp.bfloat16
    )
    hidden = jax.nn.silu(jnp.dot(mlp_mid[0], hidden, preferred_element_type=jnp.float32)).astype(
        jnp.bfloat16
    )
    hidden = jax.nn.silu(jnp.dot(mlp_mid[1], hidden, preferred_element_type=jnp.float32)).astype(
        jnp.bfloat16
    )
    output = jnp.dot(mlp_out, hidden, preferred_element_type=jnp.float32).astype(jnp.bfloat16)
    output = output.reshape(nf, levels, columns.shape[2])
    returned = lax.all_to_all(output, "lev", split_axis=1, concat_axis=2, tiled=True)
    return state + returned.astype(jnp.float32).reshape(state.shape)


class Plan:
    def __init__(self, mesh_shape, local):
        self.nf, self.levs, self.lon_dev, self.lat_dev = local
        self.lons = mesh_shape["lon"]
        self.lats = mesh_shape["lat"]
        self.zs = mesh_shape["lev"]
        self.n_lon = self.lons * self.lon_dev
        self.n_lat = self.lats * self.lat_dev
        self.jpad = round_up(self.lon_dev, 16)
        self.rows = self.lons * self.jpad
        classes = min(self.n_lon // 2 + 1, WAVES)
        self.half = round_up((classes + 1) // 2, 16)
        self.block = 2 * self.half
        self.modes = 2 * self.block
        self.degs = round_up(-(-KMAX // 2), 16)
        self.side = self.lats // 2
        self.feats = round_up(self.nf * self.levs, 8)

    def fits(self):
        plane = self.nf * self.levs * self.n_lon * self.n_lat * 4
        power_of_two = all(n & (n - 1) == 0 for n in (self.lons, self.lats, self.zs))
        return (
            SUBSTEPS == 2
            and self.nf == 3
            and power_of_two
            and plane <= PLANE_LIMIT
            and self.n_lon % 2 == 0
            and self.lats % 2 == 0
            and self.lat_dev == LANES
            and KMAX < self.n_lat
        )


def split_np(table):
    high = table.astype(np.float32).astype(jnp.bfloat16)
    low = (table - high.astype(np.float64)).astype(jnp.bfloat16)
    return high, low


def zonal_tables(plan):
    lon = np.arange(plan.n_lon)
    pos = (lon // plan.lon_dev) * plan.jpad + lon % plan.lon_dev
    scale = 2.0 / (plan.n_lon * plan.n_lat)
    ana = np.zeros((plan.modes, plan.rows))
    syn = np.zeros((plan.rows, plan.modes))
    classes = min(plan.n_lon // 2 + 1, WAVES)
    for rho in range(classes):
        phase = 2.0 * np.pi * ((rho * lon) % plan.n_lon) / plan.n_lon
        cos_row = (rho % 2) * plan.block + rho // 2
        ana[cos_row, pos] = scale * np.cos(phase)
        syn[pos, cos_row] = np.cos(phase)
        if rho > 0 and 2 * rho != plan.n_lon:
            ana[cos_row + plan.half, pos] = -scale * np.sin(phase)
            syn[pos, cos_row + plan.half] = -np.sin(phase)
    ana_h, ana_l = split_np(ana)
    syn_h, syn_l = split_np(syn)
    return (
        np.concatenate([ana_h, ana_l, ana_h], axis=1),
        np.concatenate([syn_h, syn_l, syn_h], axis=1),
    )


def meridional_tables(plan):
    lat = np.arange(plan.n_lat // 2)[None, :]
    deg = np.arange(KMAX)[:, None]
    period = 4 * plan.n_lat
    scale = np.pi / (2.0 * plan.n_lat)
    even = np.cos(((2 * lat + 1) * deg % period) * scale)
    odd = np.sin(((2 * lat + 1) * (deg + 1) % period) * scale)
    out = np.zeros((2, 2, 2, plan.degs, plan.n_lat // 2), dtype=jnp.bfloat16)
    for parity, table in enumerate((even, odd)):
        for kind in range(2):
            for part, value in enumerate(split_np(table[kind::2])):
                out[parity, kind, part, : value.shape[0]] = value
    return out


def split(value):
    high = value.astype(jnp.bfloat16)
    low = (value - high.astype(jnp.float32)).astype(jnp.bfloat16)
    return high, low


def mm(left, right):
    return lax.dot_general(
        left, right, (((1,), (0,)), ((), ())), preferred_element_type=jnp.float32
    )


def mm_l(left, right):
    return lax.dot_general(
        left, right, (((0,), (0,)), ((), ())), preferred_element_type=jnp.float32
    )


def mm_t(left, right):
    return lax.dot_general(
        left, right, (((1,), (1,)), ((), ())), preferred_element_type=jnp.float32
    )


def prepare_kernel(plan, coef_hbm, *refs):
    sources, refs = refs[:3], refs[3:]
    sv_ref, sq_ref, count_ref, gb_ref = refs[:4]
    targets, (coef_ref, sems) = refs[4:7], refs[7:]
    first = pltpu.make_async_copy(coef_hbm, coef_ref, sems.at[3])
    first.start()
    copies = [pltpu.make_async_copy(source, target, sems.at[n]) for n, (source, target) in enumerate(zip(sources, targets))]
    for copy in copies:
        copy.start()
    first.wait()
    for lev in range(plan.levs):
        gb_ref[lev] = jnp.full(gb_ref.shape[1:], coef_ref[lev, 2], jnp.float32)
    row = lax.broadcasted_iota(jnp.int32, (plan.half, plan.degs), 0)
    lane = lax.broadcasted_iota(jnp.int32, (plan.half, plan.degs), 1)
    inv_k2 = 1.0 / (KMAX * KMAX)
    turns = -(-WAVES // plan.n_lon)
    for parity in range(2):
        rho = 2 * row + parity
        terms = []
        for turn in range(turns):
            wave = rho + plan.n_lon * turn
            terms.append((wave, (wave < WAVES) & (2 * rho <= plan.n_lon)))
            wave = plan.n_lon * (turn + 1) - rho
            terms.append((wave, (wave < WAVES) & (rho > 0) & (2 * rho < plan.n_lon)))
        terms = [
            (wave.astype(jnp.float32), jnp.where(valid, jnp.where(wave == 0, 1.0, 2.0), 0.0)) for wave, valid in terms
        ]
        count_ref[parity] = sum(weight for _, weight in terms)
        for kind in range(2):
            freq = (2 * lane + kind + parity).astype(jnp.float32)
            freq2 = freq * freq
            sums = [[jnp.zeros((plan.half, plan.degs), jnp.float32) for _ in range(2)] for _ in range(plan.levs)]
            for wave, weight in terms:
                q = (wave * wave + freq2) * inv_k2
                for lev in range(plan.levs):
                    nu, ga, gb = (coef_ref[lev, i] for i in range(3))
                    hyper = nu * q * q
                    wave_q = ga * q
                    sums[lev][0] -= weight * (hyper / (1.0 + hyper))
                    sums[lev][1] += weight * (wave_q / (1.0 + gb * wave_q))
            for lev in range(plan.levs):
                sv_ref[lev, parity, kind] = sums[lev][0]
                sq_ref[lev, parity, kind] = sums[lev][1]
    for copy in copies:
        copy.wait()


def prepare(plan, coeffs):
    table = jax.ShapeDtypeStruct((plan.levs, 2, 2, plan.half, plan.degs), jnp.float32)
    vmem = pl.BlockSpec(memory_space=pltpu.VMEM)
    tables = [jnp.asarray(t) for t in (*zonal_tables(plan), meridional_tables(plan))]
    out = pl.pallas_call(
        functools.partial(prepare_kernel, plan),
        out_shape=(
            table,
            table,
            jax.ShapeDtypeStruct((2, plan.half, plan.degs), jnp.float32),
            jax.ShapeDtypeStruct((plan.levs, 8, LANES), jnp.float32),
            *(jax.ShapeDtypeStruct(t.shape, t.dtype) for t in tables),
        ),
        in_specs=[pl.BlockSpec(memory_space=pltpu.HBM)] * (1 + len(tables)),
        out_specs=(vmem,) * (4 + len(tables)),
        scratch_shapes=[pltpu.SMEM(coeffs.shape, jnp.float32), pltpu.SemaphoreType.DMA((1 + len(tables),))],
        compiler_params=pltpu.CompilerParams(vmem_limit_bytes=16 * 1024 * 1024),
        name="prepare",
    )(*[pltpu.with_memory_space_constraint(t, pltpu.HBM) for t in (coeffs, *tables)])
    return out[:4], out[4:]


def weights_kernel(plan, win_ref, mid_ref, wout_ref, w1_ref, half_ref, wo_ref):
    half_ref[...] = (0.5 * mid_ref[...].astype(jnp.float32)).astype(jnp.bfloat16)
    own_z = lax.axis_index("lev")
    total = plan.zs * plan.levs
    nin = plan.nf * total

    def feature_of(slot, count):
        block = slot // count
        inner = slot % count
        field = inner // plan.levs
        level = (own_z ^ block) * plan.levs + inner % plan.levs
        return jnp.where(inner < plan.nf * plan.levs, field * total + level, -1)

    count = plan.nf * plan.levs
    wide = plan.zs * count
    source = lax.broadcasted_iota(jnp.int32, (nin, wide), 0)
    slot = lax.broadcasted_iota(jnp.int32, (nin, wide), 1)
    pick = (source == feature_of(slot, count)).astype(jnp.float32).astype(jnp.bfloat16)
    w1_ref[...] = (0.5 * mm_l(win_ref[...], pick)).astype(jnp.bfloat16)
    slot = lax.broadcasted_iota(jnp.int32, (plan.feats, nin), 0)
    source = lax.broadcasted_iota(jnp.int32, (plan.feats, nin), 1)
    pick = (source == feature_of(slot, plan.feats)).astype(jnp.float32).astype(jnp.bfloat16)
    wo_ref[...] = mm(pick, wout_ref[...]).astype(jnp.bfloat16)


def order_weights(plan, mlp_in, mlp_mid, mlp_out):
    units = mlp_in.shape[1]
    vmem = pl.BlockSpec(memory_space=pltpu.VMEM)
    return pl.pallas_call(
        functools.partial(weights_kernel, plan),
        out_shape=(
            jax.ShapeDtypeStruct((units, plan.zs * plan.nf * plan.levs), jnp.bfloat16),
            jax.ShapeDtypeStruct(mlp_mid.shape, jnp.bfloat16),
            jax.ShapeDtypeStruct((plan.feats, units), jnp.bfloat16),
        ),
        in_specs=[vmem] * 3,
        out_specs=(vmem,) * 3,
        compiler_params=pltpu.CompilerParams(vmem_limit_bytes=16 * 1024 * 1024),
        name="order_weights",
    )(mlp_in, mlp_mid, mlp_out)


def dynamics_kernel(plan, blocks, *refs):
    block_refs = refs[:blocks]
    ana_ref, syn_ref, mer_ref, sv_ref, sq_ref, count_ref, gb_ref = refs[blocks : 7 + blocks]
    state_ref, feat_ref = refs[7 + blocks : 9 + blocks]
    grid_ref, prod_ref = refs[9 + blocks :]
    own_lon, own_lat = lax.axis_index("lon"), lax.axis_index("lat")
    nf, levs, lats = plan.nf, plan.levs, plan.lats
    block, half = plan.block, plan.half
    if plan.jpad != plan.lon_dev:
        tail = (plan.lon_dev // 8) * 8
        for lon in range(plan.lons):
            start = lon * plan.jpad + tail
            stop = (lon + 1) * plan.jpad
            zeros = jnp.zeros((stop - start, plan.lat_dev), jnp.float32)
            for side in range(2):
                for lat in range(plan.side):
                    for f in range(nf):
                        for l in range(levs):
                            grid_ref[side, lat, f, l, start:stop, :] = zeros

    def place(lat):
        south = lat >= plan.side
        return jnp.where(south, 1, 0), jnp.where(south, lats - 1 - lat, lat)

    def mirror(value, side):
        lane = lax.broadcasted_iota(jnp.int32, value.shape, 1)
        lane = jnp.where(side == 1, plan.lat_dev - 1 - lane, lane)
        return jnp.take_along_axis(value, lane, axis=1, mode="promise_in_bounds")

    for s in range(blocks):
        lon = own_lon ^ (s % plan.lons)
        side, lat = place(own_lat ^ (s // plan.lons))
        row = pl.multiple_of(lon * plan.jpad, 8)
        for f in range(nf):
            for l in range(levs):
                value = block_refs[s][f, :, l, :]
                grid_ref[side, lat, f, l, pl.ds(row, plan.lon_dev), :] = mirror(value, side)

    def whole(ref, side, *index):
        return jnp.concatenate([ref[(side, lat, *index)] for lat in range(plan.side)], axis=1)

    def analyse(values):
        middle = plan.n_lat // 2
        parts = []
        for north, south in values:
            high, low = split(jnp.concatenate([north + south, north - south], axis=1))
            parts.append(split(mm(ana_ref[...], jnp.concatenate([high, high, low], axis=0))))
        out = []
        for parity in range(2):
            kinds = []
            for kind in range(2):
                lanes = slice(kind * middle, (kind + 1) * middle)
                rows = slice(parity * block, (parity + 1) * block)
                high, low = (jnp.concatenate([part[n][rows, lanes] for part in parts], axis=0) for n in range(2))
                thigh, tlow = mer_ref[parity, kind, 0], mer_ref[parity, kind, 1]
                count = high.shape[0]
                tall = mm_t(jnp.concatenate([high, low], axis=0), thigh)
                kinds.append(tall[:count] + tall[count:] + mm_t(high, tlow))
            out.append(kinds)
        return out

    def synthesise(spectra, rows, table):
        parts = []
        for parity in range(2):
            kinds = []
            for kind in range(2):
                high, low = split(spectra[parity][kind])
                thigh, tlow = table(parity, kind)
                size = thigh.shape[1]
                if size <= LANES:
                    wide = mm(high, jnp.concatenate([thigh, tlow], axis=1))
                    kinds.append(wide[:, :size] + wide[:, size:] + mm(low, thigh))
                else:
                    kinds.append(mm(high, thigh) + mm(low, thigh) + mm(high, tlow))
            parts.append(jnp.concatenate(kinds, axis=1))
        count = spectra[0][0].shape[0] // block
        width = parts[0].shape[1] // 2
        out = []
        for n in range(count):
            both = jnp.concatenate([part[n * block : (n + 1) * block] for part in parts], axis=0)
            high, low = split(both)
            grid = mm(rows, jnp.concatenate([high, high, low], axis=0))
            out.append((grid[:, :width], grid[:, width:]))
        return out

    def at(spectrum, f, l):
        n = f * levs + l
        return spectrum[n * block : (n + 1) * block]

    pairs = [(parity, kind) for parity in range(2) for kind in range(2)]
    lane = lax.broadcasted_iota(jnp.int32, (block, plan.degs), 1)
    cls = lax.broadcasted_iota(jnp.int32, (block, plan.degs), 0) % half
    norms, counts = {}, {}
    for parity in range(2):
        rho = 2 * cls + parity
        alone = (rho == 0) | (2 * rho == plan.n_lon)
        norm = jnp.where(alone, 1.0, 0.5)
        weight = jnp.concatenate([count_ref[parity]] * 2, axis=0)
        for kind in range(2):
            counts[parity, kind] = weight
            norms[parity, kind] = norm * jnp.where(lane == 0, 2.0, 1.0) if parity == kind == 0 else norm

    def changes(spectra):
        out = {}
        for pair in pairs:
            per = [[None] * levs for _ in range(nf)]
            for l in range(levs):
                sv = jnp.concatenate([sv_ref[(l, *pair)]] * 2, axis=0)
                sq = jnp.concatenate([sq_ref[(l, *pair)]] * 2, axis=0)
                gb = gb_ref[l, 0:1, 0:1]
                vort, diverg, temper = (spectra[pair][f][l] for f in range(3))
                per[0][l] = sv * vort
                per[1][l] = sq * (temper - gb * diverg)
                per[2][l] = -gb * (counts[pair] * diverg + per[1][l])
            out[pair] = per
        return out

    def stack(nested, fields):
        return [
            [
                jnp.concatenate([nested[parity, kind][f][l] for f in fields for l in range(levs)], axis=0)
                for kind in range(2)
            ]
            for parity in range(2)
        ]

    flat = analyse([tuple(whole(grid_ref, side, f, l) for side in range(2)) for f in range(nf) for l in range(levs)])
    spectra = {
        (parity, kind): [[at(flat[parity][kind], f, l) for l in range(levs)] for f in range(nf)]
        for parity, kind in pairs
    }
    first = changes(spectra)
    grown = synthesise(
        stack(first, (0, 1)), syn_ref[...], lambda parity, kind: (mer_ref[parity, kind, 0], mer_ref[parity, kind, 1])
    )
    products = []
    for l in range(levs):
        (vsym, vanti), (dsym, danti) = grown[l], grown[levs + l]
        sides = []
        for side in range(2):
            vort = whole(grid_ref, side, 0, l) + (vsym - vanti if side else vsym + vanti)
            diverg = whole(grid_ref, side, 1, l) + (dsym - danti if side else dsym + danti)
            product = 0.25 * vort * diverg
            for lat in range(plan.side):
                prod_ref[side, lat, l] = product[:, lat * plan.lat_dev : (lat + 1) * plan.lat_dev]
            sides.append(product)
        products.append(tuple(sides))
    extra = analyse(products)
    updated = {}
    for pair in pairs:
        per = [[spectra[pair][f][l] + norms[pair] * first[pair][f][l] for l in range(levs)] for f in range(nf)]
        per[2] = [per[2][l] + at(extra[pair[0]][pair[1]], 0, l) for l in range(levs)]
        updated[pair] = per
    second = changes(updated)
    both = {
        pair: [[first[pair][f][l] + second[pair][f][l] for l in range(levs)] for f in range(nf)] for pair in pairs
    }
    side, lat = place(own_lat)
    own_start = pl.multiple_of(lat * plan.lat_dev, LANES)
    own_row = pl.multiple_of(own_lon * plan.jpad, 8)
    own = synthesise(
        stack(both, range(nf)),
        syn_ref[pl.ds(own_row, plan.jpad), :],
        lambda parity, kind: tuple(mer_ref[parity, kind, part, :, pl.ds(own_start, plan.lat_dev)] for part in range(2)),
    )
    sign = jnp.where(side == 1, -1.0, 1.0)
    for l in range(levs):
        vort, diverg, temper = (
            grid_ref[side, lat, f, l, pl.ds(own_row, plan.jpad), :]
            + (own[f * levs + l][0] + sign * own[f * levs + l][1])
            for f in range(3)
        )
        temper = temper + prod_ref[side, lat, l, pl.ds(own_row, plan.jpad), :] + 0.25 * vort * diverg
        for f, value in enumerate((vort, diverg, temper)):
            value = mirror(value, side)
            state_ref[f, l] = value[: plan.lon_dev]
            feat_ref[f * levs + l] = value.astype(jnp.bfloat16)


def dynamics(plan, blocks, tables, sums):
    vmem = pl.BlockSpec(memory_space=pltpu.VMEM)
    return pl.pallas_call(
        functools.partial(dynamics_kernel, plan, len(blocks)),
        out_shape=(
            jax.ShapeDtypeStruct((plan.nf, plan.levs, plan.lon_dev, plan.lat_dev), jnp.float32),
            jax.ShapeDtypeStruct((plan.nf * plan.levs, plan.jpad, plan.lat_dev), jnp.bfloat16),
        ),
        in_specs=[vmem] * (len(blocks) + 7),
        out_specs=(vmem,) * 2,
        scratch_shapes=[
            pltpu.VMEM((2, plan.side, plan.nf, plan.levs, plan.rows, plan.lat_dev), jnp.float32),
            pltpu.VMEM((2, plan.side, plan.levs, plan.rows, plan.lat_dev), jnp.float32),
        ],
        compiler_params=pltpu.CompilerParams(vmem_limit_bytes=32 * 1024 * 1024),
        name="dynamics",
    )(*blocks, *tables, *sums)


def silu_of_half(half):
    return (half + half * jnp.tanh(half)).astype(jnp.bfloat16)


def network_kernel(plan, blocks, groups, *refs):
    block_refs = refs[:blocks]
    w1_ref, mid_ref, wo_ref, state_ref, out_ref, wide_ref, tile_ref, sum_ref, sems = refs[blocks:]
    features = plan.nf * plan.levs
    rows = features * plan.jpad
    for s, ref in enumerate(block_refs):
        wide_ref[s * rows : (s + 1) * rows, :] = ref[...].astype(jnp.float32).reshape(rows, plan.lat_dev)
    copies = []
    for number, (start, stop) in enumerate(groups):
        inputs = jnp.concatenate(
            [
                wide_ref[pl.ds(lon, blocks * features, stride=plan.jpad), :].astype(jnp.bfloat16)
                for lon in range(start, stop)
            ],
            axis=1,
        )
        hidden = silu_of_half(mm(w1_ref[...], inputs))
        hidden = silu_of_half(mm(mid_ref[0], hidden))
        hidden = silu_of_half(mm(mid_ref[1], hidden))
        output = mm(wo_ref[...], hidden).astype(jnp.bfloat16).astype(jnp.float32)
        for lon in range(start, stop):
            tile_ref[lon] = output[:, (lon - start) * plan.lat_dev : (lon - start + 1) * plan.lat_dev]
        for f in range(plan.nf):
            for l in range(plan.levs):
                correction = tile_ref[start:stop, f * plan.levs + l, :]
                sum_ref[f, start:stop, l, :] = state_ref[f, l, start:stop, :] + correction
            part = (f, pl.ds(start, stop - start))
            copy = pltpu.make_async_copy(sum_ref.at[part], out_ref.at[part], sems.at[number, f])
            copy.start()
            copies.append(copy)
    for copy in copies:
        copy.wait()


def network(plan, state, blocks, weights):
    vmem = pl.BlockSpec(memory_space=pltpu.VMEM)
    size = max(1, GROUP // plan.lat_dev)
    groups = [(start, min(start + size, plan.lon_dev)) for start in range(0, plan.lon_dev, size)]
    out = jax.ShapeDtypeStruct((plan.nf, plan.lon_dev, plan.levs, plan.lat_dev), jnp.float32)
    return pl.pallas_call(
        functools.partial(network_kernel, plan, len(blocks), groups),
        out_shape=out,
        in_specs=[vmem] * (len(blocks) + 4),
        out_specs=pl.BlockSpec(memory_space=pltpu.HBM),
        scratch_shapes=[
            pltpu.VMEM((len(blocks) * plan.nf * plan.levs * plan.jpad, plan.lat_dev), jnp.float32),
            pltpu.VMEM((plan.lon_dev, plan.feats, plan.lat_dev), jnp.float32),
            pltpu.VMEM(out.shape, jnp.float32),
            pltpu.SemaphoreType.DMA((len(groups), plan.nf)),
        ],
        compiler_params=pltpu.CompilerParams(vmem_limit_bytes=24 * 1024 * 1024),
        name="network",
    )(*blocks, *weights, state)


def swap(value, axes, sizes, mask):
    count = int(np.prod(sizes))
    return lax.ppermute(value, axes, [(i, i ^ mask) for i in range(count)])


def gathering(plan, fields, spectral_coeffs, mlp_in, mlp_mid, mlp_out):
    fields = fields.transpose(0, 2, 1, 3)
    plane = ("lon", "lat")
    sizes = (plan.lons, plan.lats)
    blocks = [None] * (plan.lons * plan.lats)
    outer = [(lon, lat) for lat in range(0, plan.lats, 2) for lon in range(plan.lons)]
    for lon, lat in outer:
        mask = lon * plan.lats + lat
        blocks[lat * plan.lons + lon] = swap(fields, plane, sizes, mask) if mask else fields
    if plan.lats > 1:
        for lon, lat in outer:
            blocks[(lat ^ 1) * plan.lons + lon] = swap(blocks[lat * plan.lons + lon], plane, sizes, 1)
    sums, tables = prepare(plan, spectral_coeffs.T)
    weights = order_weights(plan, mlp_in.T, mlp_mid, mlp_out)
    state, feats = dynamics(plan, blocks, tables, sums)
    parts = [feats]
    for mask in range(1, plan.zs):
        parts.append(swap(feats, ("lev",), (plan.zs,), mask))
    return network(plan, state, parts, weights).transpose(0, 2, 1, 3)


def solution(mesh):
    in_specs = (P(None, "lev", "lon", "lat"), P(None, "lev"), P(), P(), P())
    out_specs = P(None, "lev", "lon", "lat")

    def per_device(fields, spectral_coeffs, mlp_in, mlp_mid, mlp_out):
        plan = Plan(mesh.shape, fields.shape)
        if plan.fits():
            return gathering(plan, fields, spectral_coeffs, mlp_in, mlp_mid, mlp_out)
        return transposing(fields, spectral_coeffs, mlp_in, mlp_mid, mlp_out)

    def step(fields, *rest):
        return jax.shard_map(
            per_device, mesh=mesh, in_specs=in_specs, out_specs=out_specs, check_vma=False
        )(fields, *rest)

    return step
```

```python
import functools

import jax
import jax.numpy as jnp
import numpy as np
from jax import lax
from jax.experimental import pallas as pl
from jax.experimental.pallas import tpu as pltpu
from jax.sharding import PartitionSpec as P


WAVES = 320
KMAX = 320
SUBSTEPS = 2


highest = lax.Precision.HIGHEST
LANES = 128
GROUP = 2048
PLANE_LIMIT = 4 * 1024 * 1024


def round_up(value, unit):
    return -(-value // unit) * unit


def forward_table(lon_ids, total_lon, waves):
    wave_ids = jnp.arange(waves, dtype=jnp.int32)
    phase = (lon_ids[:, None] * wave_ids[None, :] % total_lon).astype(jnp.float32) * (
        2.0 * jnp.pi / total_lon
    )
    return jnp.concatenate([jnp.cos(phase), -jnp.sin(phase)], axis=1) / total_lon


def inverse_table(lon_ids, total_lon, waves):
    wave_ids = jnp.arange(waves, dtype=jnp.int32)
    phase = (wave_ids[:, None] * lon_ids[None, :] % total_lon).astype(jnp.float32) * (
        2.0 * jnp.pi / total_lon
    )
    weight = jnp.where(wave_ids == 0, 1.0, 2.0).astype(jnp.float32)[:, None]
    return jnp.concatenate([weight * jnp.cos(phase), -weight * jnp.sin(phase)], axis=0)


def latitude_tables(lat_ids, total_lat, degree_ids):
    odd_rows = 2 * lat_ids[:, None] + 1
    period = 4 * total_lat
    scale = jnp.pi / (2.0 * total_lat)
    even_arg = (odd_rows * degree_ids[None, :] % period).astype(jnp.float32) * scale
    odd_arg = (odd_rows * (degree_ids[None, :] + 1) % period).astype(jnp.float32) * scale
    return (jnp.cos(even_arg), jnp.sin(odd_arg))


def latitude_forward(waves, even_tab, odd_tab):
    cols, nf, levs, lats = waves.shape
    pairs = waves.reshape(cols // 2, 2, nf, levs, lats)
    even_part = jnp.einsum("pfli,ik->pflk", pairs[:, 0], even_tab, precision=highest)
    odd_part = jnp.einsum("pfli,ik->pflk", pairs[:, 1], odd_tab, precision=highest)
    return jnp.stack([even_part, odd_part], axis=1).reshape(cols, nf, levs, even_tab.shape[1])


def latitude_inverse(spectra, even_tab, odd_tab):
    cols, nf, levs, degs = spectra.shape
    pairs = spectra.reshape(cols // 2, 2, nf, levs, degs)
    even_part = jnp.einsum("pflk,ik->pfli", pairs[:, 0], even_tab, precision=highest)
    odd_part = jnp.einsum("pflk,ik->pfli", pairs[:, 1], odd_tab, precision=highest)
    return jnp.stack([even_part, odd_part], axis=1).reshape(cols, nf, levs, even_tab.shape[0])


def operator(spectra, coeffs, col_waves, degree_ids):
    parity = col_waves % 2
    freq = (degree_ids[None, :] + parity[:, None]).astype(jnp.float32)
    wavenum = col_waves.astype(jnp.float32)[:, None]
    qvalue = ((wavenum * wavenum + freq * freq) / (KMAX * KMAX))[:, None, :]
    hyper = coeffs[0][None, :, None]
    coupling = coeffs[1][None, :, None]
    depth = coeffs[2][None, :, None]
    vort = spectra[:, 0]
    diverg = spectra[:, 1]
    temper = spectra[:, 2]
    new_vort = vort / (1.0 + hyper * qvalue * qvalue)
    new_div = (diverg + coupling * qvalue * temper) / (1.0 + coupling * depth * qvalue)
    new_temp = temper - depth * new_div
    return jnp.stack([new_vort - vort, new_div - diverg, new_temp - temper], axis=1)


def nonlinear(state):
    temper = state[2] + 0.25 * state[0] * state[1]
    return jnp.stack([state[0], state[1], temper], axis=0)


def transposing(fields, spectral_coeffs, mlp_in, mlp_mid, mlp_out):
    nf, lev_dev, lon_dev, lat_dev = fields.shape
    lon_count = lax.axis_size("lon")
    lat_count = lax.axis_size("lat")
    total_lon = lon_dev * lon_count
    total_lat = lat_dev * lat_count
    wave_cols = 2 * WAVES // lon_count
    row_count = nf * lev_dev * lat_dev
    lat_ids = lax.axis_index("lat") * lat_dev + jnp.arange(lat_dev, dtype=jnp.int32)
    col_waves = (lax.axis_index("lon") * wave_cols + jnp.arange(wave_cols, dtype=jnp.int32)) % WAVES
    weight = 2.0 / total_lat
    all_lons = jnp.arange(total_lon, dtype=jnp.int32)
    fwd_full = forward_table(all_lons, total_lon, WAVES)
    inv_full = inverse_table(all_lons, total_lon, WAVES)
    own_degrees = jnp.arange(KMAX, dtype=jnp.int32)
    full_even, full_odd = latitude_tables(lat_ids, total_lat, own_degrees)
    state = fields
    for _ in range(SUBSTEPS):
        flat = state.transpose(0, 1, 3, 2).reshape(row_count, lon_dev)
        by_row = lax.all_to_all(flat, "lon", split_axis=0, concat_axis=1, tiled=True)
        row_waves = jnp.dot(by_row, fwd_full, precision=highest)
        by_col = lax.all_to_all(row_waves, "lon", split_axis=1, concat_axis=0, tiled=True)
        waves = by_col.reshape(nf, lev_dev, lat_dev, wave_cols).transpose(3, 0, 1, 2)
        partial_spectra = latitude_forward(waves, full_even * weight, full_odd * weight)
        spectra = lax.psum(partial_spectra, "lat")
        change = operator(spectra, spectral_coeffs, col_waves, own_degrees)
        back = latitude_inverse(change, full_even, full_odd)
        flat_back = back.transpose(1, 2, 3, 0).reshape(row_count, wave_cols)
        full_waves = lax.all_to_all(flat_back, "lon", split_axis=0, concat_axis=1, tiled=True)
        row_grid = jnp.dot(full_waves, inv_full, precision=highest)
        own_grid = lax.all_to_all(row_grid, "lon", split_axis=1, concat_axis=0, tiled=True)
        increment = own_grid.reshape(nf, lev_dev, lat_dev, lon_dev).transpose(0, 1, 3, 2)
        state = nonlinear(state + increment)
    features = state.astype(jnp.bfloat16).reshape(nf, lev_dev, lon_dev * lat_dev)
    columns = lax.all_to_all(features, "lev", split_axis=2, concat_axis=1, tiled=True)
    levels = columns.shape[1]
    inputs = columns.reshape(nf * levels, columns.shape[2])
    hidden = jax.nn.silu(jnp.dot(mlp_in, inputs, preferred_element_type=jnp.float32)).astype(
        jnp.bfloat16
    )
    hidden = jax.nn.silu(jnp.dot(mlp_mid[0], hidden, preferred_element_type=jnp.float32)).astype(
        jnp.bfloat16
    )
    hidden = jax.nn.silu(jnp.dot(mlp_mid[1], hidden, preferred_element_type=jnp.float32)).astype(
        jnp.bfloat16
    )
    output = jnp.dot(mlp_out, hidden, preferred_element_type=jnp.float32).astype(jnp.bfloat16)
    output = output.reshape(nf, levels, columns.shape[2])
    returned = lax.all_to_all(output, "lev", split_axis=1, concat_axis=2, tiled=True)
    return state + returned.astype(jnp.float32).reshape(state.shape)


class Plan:
    def __init__(self, mesh_shape, local):
        self.nf, self.levs, self.lon_dev, self.lat_dev = local
        self.lons = mesh_shape["lon"]
        self.lats = mesh_shape["lat"]
        self.zs = mesh_shape["lev"]
        self.n_lon = self.lons * self.lon_dev
        self.n_lat = self.lats * self.lat_dev
        self.jpad = round_up(self.lon_dev, 16)
        self.rows = self.lons * self.jpad
        classes = min(self.n_lon // 2 + 1, WAVES)
        self.half = round_up((classes + 1) // 2, 16)
        self.block = 2 * self.half
        self.modes = 2 * self.block
        self.degs = round_up(-(-KMAX // 2), 16)
        self.side = self.lats // 2
        self.feats = round_up(self.nf * self.levs, 8)

    def fits(self):
        plane = self.nf * self.levs * self.n_lon * self.n_lat * 4
        power_of_two = all(n & (n - 1) == 0 for n in (self.lons, self.lats, self.zs))
        return (
            SUBSTEPS == 2
            and self.nf == 3
            and power_of_two
            and plane <= PLANE_LIMIT
            and self.n_lon % 2 == 0
            and self.lats % 2 == 0
            and self.lat_dev == LANES
            and KMAX < self.n_lat
        )


def split_np(table):
    high = table.astype(np.float32).astype(jnp.bfloat16)
    low = (table - high.astype(np.float64)).astype(jnp.bfloat16)
    return high, low


def zonal_tables(plan):
    lon = np.arange(plan.n_lon)
    pos = (lon // plan.lon_dev) * plan.jpad + lon % plan.lon_dev
    scale = 2.0 / (plan.n_lon * plan.n_lat)
    ana = np.zeros((plan.modes, plan.rows))
    syn = np.zeros((plan.rows, plan.modes))
    classes = min(plan.n_lon // 2 + 1, WAVES)
    for rho in range(classes):
        phase = 2.0 * np.pi * ((rho * lon) % plan.n_lon) / plan.n_lon
        cos_row = (rho % 2) * plan.block + rho // 2
        ana[cos_row, pos] = scale * np.cos(phase)
        syn[pos, cos_row] = np.cos(phase)
        if rho > 0 and 2 * rho != plan.n_lon:
            ana[cos_row + plan.half, pos] = -scale * np.sin(phase)
            syn[pos, cos_row + plan.half] = -np.sin(phase)
    ana_h, ana_l = split_np(ana)
    syn_h, syn_l = split_np(syn)
    return (
        np.concatenate([ana_h, ana_l, ana_h], axis=1),
        np.concatenate([syn_h, syn_l, syn_h], axis=1),
    )


def meridional_tables(plan):
    lat = np.arange(plan.n_lat // 2)[None, :]
    deg = np.arange(KMAX)[:, None]
    period = 4 * plan.n_lat
    scale = np.pi / (2.0 * plan.n_lat)
    even = np.cos(((2 * lat + 1) * deg % period) * scale)
    odd = np.sin(((2 * lat + 1) * (deg + 1) % period) * scale)
    out = np.zeros((2, 2, 2, plan.degs, plan.n_lat // 2), dtype=jnp.bfloat16)
    for parity, table in enumerate((even, odd)):
        for kind in range(2):
            for part, value in enumerate(split_np(table[kind::2])):
                out[parity, kind, part, : value.shape[0]] = value
    return out


def split(value):
    high = value.astype(jnp.bfloat16)
    low = (value - high.astype(jnp.float32)).astype(jnp.bfloat16)
    return high, low


def mm(left, right):
    return lax.dot_general(
        left, right, (((1,), (0,)), ((), ())), preferred_element_type=jnp.float32
    )


def mm_l(left, right):
    return lax.dot_general(
        left, right, (((0,), (0,)), ((), ())), preferred_element_type=jnp.float32
    )


def mm_t(left, right):
    return lax.dot_general(
        left, right, (((1,), (1,)), ((), ())), preferred_element_type=jnp.float32
    )


def prepare_kernel(plan, coef_hbm, *refs):
    sources, refs = refs[:3], refs[3:]
    sv_ref, sq_ref, count_ref, gb_ref = refs[:4]
    targets, (coef_ref, sems) = refs[4:7], refs[7:]
    first = pltpu.make_async_copy(coef_hbm, coef_ref, sems.at[3])
    first.start()
    copies = [pltpu.make_async_copy(source, target, sems.at[n]) for n, (source, target) in enumerate(zip(sources, targets))]
    for copy in copies:
        copy.start()
    first.wait()
    for lev in range(plan.levs):
        gb_ref[lev] = jnp.full(gb_ref.shape[1:], coef_ref[lev, 2], jnp.float32)
    row = lax.broadcasted_iota(jnp.int32, (plan.half, plan.degs), 0)
    lane = lax.broadcasted_iota(jnp.int32, (plan.half, plan.degs), 1)
    inv_k2 = 1.0 / (KMAX * KMAX)
    turns = -(-WAVES // plan.n_lon)
    for parity in range(2):
        rho = 2 * row + parity
        terms = []
        for turn in range(turns):
            wave = rho + plan.n_lon * turn
            terms.append((wave, (wave < WAVES) & (2 * rho <= plan.n_lon)))
            wave = plan.n_lon * (turn + 1) - rho
            terms.append((wave, (wave < WAVES) & (rho > 0) & (2 * rho < plan.n_lon)))
        terms = [
            (wave.astype(jnp.float32), jnp.where(valid, jnp.where(wave == 0, 1.0, 2.0), 0.0)) for wave, valid in terms
        ]
        count_ref[parity] = sum(weight for _, weight in terms)
        for kind in range(2):
            freq = (2 * lane + kind + parity).astype(jnp.float32)
            freq2 = freq * freq
            sums = [[jnp.zeros((plan.half, plan.degs), jnp.float32) for _ in range(2)] for _ in range(plan.levs)]
            for wave, weight in terms:
                q = (wave * wave + freq2) * inv_k2
                for lev in range(plan.levs):
                    nu, ga, gb = (coef_ref[lev, i] for i in range(3))
                    hyper = nu * q * q
                    wave_q = ga * q
                    sums[lev][0] -= weight * (hyper / (1.0 + hyper))
                    sums[lev][1] += weight * (wave_q / (1.0 + gb * wave_q))
            for lev in range(plan.levs):
                sv_ref[lev, parity, kind] = sums[lev][0]
                sq_ref[lev, parity, kind] = sums[lev][1]
    for copy in copies:
        copy.wait()


def prepare(plan, coeffs):
    table = jax.ShapeDtypeStruct((plan.levs, 2, 2, plan.half, plan.degs), jnp.float32)
    vmem = pl.BlockSpec(memory_space=pltpu.VMEM)
    tables = [jnp.asarray(t) for t in (*zonal_tables(plan), meridional_tables(plan))]
    out = pl.pallas_call(
        functools.partial(prepare_kernel, plan),
        out_shape=(
            table,
            table,
            jax.ShapeDtypeStruct((2, plan.half, plan.degs), jnp.float32),
            jax.ShapeDtypeStruct((plan.levs, 8, LANES), jnp.float32),
            *(jax.ShapeDtypeStruct(t.shape, t.dtype) for t in tables),
        ),
        in_specs=[pl.BlockSpec(memory_space=pltpu.HBM)] * (1 + len(tables)),
        out_specs=(vmem,) * (4 + len(tables)),
        scratch_shapes=[pltpu.SMEM(coeffs.shape, jnp.float32), pltpu.SemaphoreType.DMA((1 + len(tables),))],
        compiler_params=pltpu.CompilerParams(vmem_limit_bytes=16 * 1024 * 1024),
        name="prepare",
    )(*[pltpu.with_memory_space_constraint(t, pltpu.HBM) for t in (coeffs, *tables)])
    return out[:4], out[4:]


def weights_kernel(plan, win_ref, mid_ref, wout_ref, w1_ref, half_ref, wo_ref):
    half_ref[...] = (0.5 * mid_ref[...].astype(jnp.float32)).astype(jnp.bfloat16)
    own_z = lax.axis_index("lev")
    total = plan.zs * plan.levs
    nin = plan.nf * total

    def feature_of(slot, count):
        block = slot // count
        inner = slot % count
        field = inner // plan.levs
        level = (own_z ^ block) * plan.levs + inner % plan.levs
        return jnp.where(inner < plan.nf * plan.levs, field * total + level, -1)

    count = plan.nf * plan.levs
    wide = plan.zs * count
    source = lax.broadcasted_iota(jnp.int32, (nin, wide), 0)
    slot = lax.broadcasted_iota(jnp.int32, (nin, wide), 1)
    pick = (source == feature_of(slot, count)).astype(jnp.float32).astype(jnp.bfloat16)
    w1_ref[...] = (0.5 * mm_l(win_ref[...], pick)).astype(jnp.bfloat16)
    slot = lax.broadcasted_iota(jnp.int32, (plan.feats, nin), 0)
    source = lax.broadcasted_iota(jnp.int32, (plan.feats, nin), 1)
    pick = (source == feature_of(slot, plan.feats)).astype(jnp.float32).astype(jnp.bfloat16)
    wo_ref[...] = mm(pick, wout_ref[...]).astype(jnp.bfloat16)


def order_weights(plan, mlp_in, mlp_mid, mlp_out):
    units = mlp_in.shape[1]
    vmem = pl.BlockSpec(memory_space=pltpu.VMEM)
    return pl.pallas_call(
        functools.partial(weights_kernel, plan),
        out_shape=(
            jax.ShapeDtypeStruct((units, plan.zs * plan.nf * plan.levs), jnp.bfloat16),
            jax.ShapeDtypeStruct(mlp_mid.shape, jnp.bfloat16),
            jax.ShapeDtypeStruct((plan.feats, units), jnp.bfloat16),
        ),
        in_specs=[vmem] * 3,
        out_specs=(vmem,) * 3,
        compiler_params=pltpu.CompilerParams(vmem_limit_bytes=16 * 1024 * 1024),
        name="order_weights",
    )(mlp_in, mlp_mid, mlp_out)


def dynamics_kernel(plan, blocks, *refs):
    block_refs = refs[:blocks]
    ana_ref, syn_ref, mer_ref, sv_ref, sq_ref, count_ref, gb_ref = refs[blocks : 7 + blocks]
    state_ref, feat_ref = refs[7 + blocks : 9 + blocks]
    grid_ref, prod_ref, pack_ref = refs[9 + blocks :]
    own_lon, own_lat = lax.axis_index("lon"), lax.axis_index("lat")
    nf, levs, lats = plan.nf, plan.levs, plan.lats
    block, half = plan.block, plan.half
    if plan.jpad != plan.lon_dev:
        tail = (plan.lon_dev // 8) * 8
        for lon in range(plan.lons):
            start = lon * plan.jpad + tail
            stop = (lon + 1) * plan.jpad
            zeros = jnp.zeros((stop - start, plan.lat_dev), jnp.float32)
            for side in range(2):
                for lat in range(plan.side):
                    for f in range(nf):
                        for l in range(levs):
                            grid_ref[side, lat, f, l, start:stop, :] = zeros

    def place(lat):
        south = lat >= plan.side
        return jnp.where(south, 1, 0), jnp.where(south, lats - 1 - lat, lat)

    def mirror(value, side):
        lane = lax.broadcasted_iota(jnp.int32, value.shape, 1)
        lane = jnp.where(side == 1, plan.lat_dev - 1 - lane, lane)
        return jnp.take_along_axis(value, lane, axis=1, mode="promise_in_bounds")

    for s in range(blocks):
        lon = own_lon ^ (s % plan.lons)
        side, lat = place(own_lat ^ (s // plan.lons))
        row = pl.multiple_of(lon * plan.jpad, 8)
        for f in range(nf):
            for l in range(levs):
                value = block_refs[s][f, :, l, :]
                grid_ref[side, lat, f, l, pl.ds(row, plan.lon_dev), :] = mirror(value, side)

    def whole(ref, side, *index):
        return jnp.concatenate([ref[(side, lat, *index)] for lat in range(plan.side)], axis=1)

    def analyse(values):
        middle = plan.n_lat // 2
        parts = []
        for north, south in values:
            high, low = split(jnp.concatenate([north + south, north - south], axis=1))
            parts.append(split(mm(ana_ref[...], jnp.concatenate([high, high, low], axis=0))))
        out = []
        for parity in range(2):
            kinds = []
            for kind in range(2):
                lanes = slice(kind * middle, (kind + 1) * middle)
                rows = slice(parity * block, (parity + 1) * block)
                high, low = (jnp.concatenate([part[n][rows, lanes] for part in parts], axis=0) for n in range(2))
                thigh, tlow = mer_ref[parity, kind, 0], mer_ref[parity, kind, 1]
                count = high.shape[0]
                tall = mm_t(jnp.concatenate([high, low], axis=0), thigh)
                kinds.append(tall[:count] + tall[count:] + mm_t(high, tlow))
            out.append(kinds)
        return out

    def synthesise(spectra, rows, table):
        parts = []
        for parity in range(2):
            kinds = []
            for kind in range(2):
                high, low = split(spectra[parity][kind])
                thigh, tlow = table(parity, kind)
                size = thigh.shape[1]
                if size <= LANES:
                    wide = mm(high, jnp.concatenate([thigh, tlow], axis=1))
                    kinds.append(wide[:, :size] + wide[:, size:] + mm(low, thigh))
                else:
                    kinds.append(mm(high, thigh) + mm(low, thigh) + mm(high, tlow))
            parts.append(jnp.concatenate(kinds, axis=1))
        count = spectra[0][0].shape[0] // block
        width = parts[0].shape[1] // 2
        out = []
        for n in range(count):
            both = jnp.concatenate([part[n * block : (n + 1) * block] for part in parts], axis=0)
            high, low = split(both)
            grid = mm(rows, jnp.concatenate([high, high, low], axis=0))
            out.append((grid[:, :width], grid[:, width:]))
        return out

    def at(spectrum, f, l):
        n = f * levs + l
        return spectrum[n * block : (n + 1) * block]

    pairs = [(parity, kind) for parity in range(2) for kind in range(2)]
    lane = lax.broadcasted_iota(jnp.int32, (block, plan.degs), 1)
    cls = lax.broadcasted_iota(jnp.int32, (block, plan.degs), 0) % half
    norms, counts = {}, {}
    for parity in range(2):
        rho = 2 * cls + parity
        alone = (rho == 0) | (2 * rho == plan.n_lon)
        norm = jnp.where(alone, 1.0, 0.5)
        weight = jnp.concatenate([count_ref[parity]] * 2, axis=0)
        for kind in range(2):
            counts[parity, kind] = weight
            norms[parity, kind] = norm * jnp.where(lane == 0, 2.0, 1.0) if parity == kind == 0 else norm

    def changes(spectra):
        out = {}
        for pair in pairs:
            per = [[None] * levs for _ in range(nf)]
            for l in range(levs):
                sv = jnp.concatenate([sv_ref[(l, *pair)]] * 2, axis=0)
                sq = jnp.concatenate([sq_ref[(l, *pair)]] * 2, axis=0)
                gb = gb_ref[l, 0:1, 0:1]
                vort, diverg, temper = (spectra[pair][f][l] for f in range(3))
                per[0][l] = sv * vort
                per[1][l] = sq * (temper - gb * diverg)
                per[2][l] = -gb * (counts[pair] * diverg + per[1][l])
            out[pair] = per
        return out

    def stack(nested, fields):
        return [
            [
                jnp.concatenate([nested[parity, kind][f][l] for f in fields for l in range(levs)], axis=0)
                for kind in range(2)
            ]
            for parity in range(2)
        ]

    flat = analyse([tuple(whole(grid_ref, side, f, l) for side in range(2)) for f in range(nf) for l in range(levs)])
    spectra = {
        (parity, kind): [[at(flat[parity][kind], f, l) for l in range(levs)] for f in range(nf)]
        for parity, kind in pairs
    }
    first = changes(spectra)
    grown = synthesise(
        stack(first, (0, 1)), syn_ref[...], lambda parity, kind: (mer_ref[parity, kind, 0], mer_ref[parity, kind, 1])
    )
    products = []
    for l in range(levs):
        (vsym, vanti), (dsym, danti) = grown[l], grown[levs + l]
        sides = []
        for side in range(2):
            vort = whole(grid_ref, side, 0, l) + (vsym - vanti if side else vsym + vanti)
            diverg = whole(grid_ref, side, 1, l) + (dsym - danti if side else dsym + danti)
            product = 0.25 * vort * diverg
            for lat in range(plan.side):
                prod_ref[side, lat, l] = product[:, lat * plan.lat_dev : (lat + 1) * plan.lat_dev]
            sides.append(product)
        products.append(tuple(sides))
    extra = analyse(products)
    updated = {}
    for pair in pairs:
        per = [[spectra[pair][f][l] + norms[pair] * first[pair][f][l] for l in range(levs)] for f in range(nf)]
        per[2] = [per[2][l] + at(extra[pair[0]][pair[1]], 0, l) for l in range(levs)]
        updated[pair] = per
    second = changes(updated)
    both = {
        pair: [[first[pair][f][l] + second[pair][f][l] for l in range(levs)] for f in range(nf)] for pair in pairs
    }
    side, lat = place(own_lat)
    own_start = pl.multiple_of(lat * plan.lat_dev, LANES)
    own_row = pl.multiple_of(own_lon * plan.jpad, 8)
    own = synthesise(
        stack(both, range(nf)),
        syn_ref[pl.ds(own_row, plan.jpad), :],
        lambda parity, kind: tuple(mer_ref[parity, kind, part, :, pl.ds(own_start, plan.lat_dev)] for part in range(2)),
    )
    sign = jnp.where(side == 1, -1.0, 1.0)
    for l in range(levs):
        vort, diverg, temper = (
            grid_ref[side, lat, f, l, pl.ds(own_row, plan.jpad), :]
            + (own[f * levs + l][0] + sign * own[f * levs + l][1])
            for f in range(3)
        )
        temper = temper + prod_ref[side, lat, l, pl.ds(own_row, plan.jpad), :] + 0.25 * vort * diverg
        for f, value in enumerate((vort, diverg, temper)):
            value = mirror(value, side)
            state_ref[f, l] = value[: plan.lon_dev]
            start = (f * levs + l) * plan.lon_dev
            pack_ref[start : start + plan.lon_dev, :] = value[: plan.lon_dev]
    feat_ref[...] = pack_ref[: feat_ref.shape[0], :].astype(jnp.bfloat16)


def dynamics(plan, blocks, tables, sums):
    vmem = pl.BlockSpec(memory_space=pltpu.VMEM)
    return pl.pallas_call(
        functools.partial(dynamics_kernel, plan, len(blocks)),
        out_shape=(
            jax.ShapeDtypeStruct((plan.nf, plan.levs, plan.lon_dev, plan.lat_dev), jnp.float32),
            jax.ShapeDtypeStruct((plan.nf * plan.levs * plan.lon_dev, plan.lat_dev), jnp.bfloat16),
        ),
        in_specs=[vmem] * (len(blocks) + 7),
        out_specs=(vmem,) * 2,
        scratch_shapes=[
            pltpu.VMEM((2, plan.side, plan.nf, plan.levs, plan.rows, plan.lat_dev), jnp.float32),
            pltpu.VMEM((2, plan.side, plan.levs, plan.rows, plan.lat_dev), jnp.float32),
            pltpu.VMEM((round_up(plan.nf * plan.levs * plan.lon_dev, 8) + 8, plan.lat_dev), jnp.float32),
        ],
        compiler_params=pltpu.CompilerParams(vmem_limit_bytes=32 * 1024 * 1024),
        name="dynamics",
    )(*blocks, *tables, *sums)


def silu_of_half(half):
    return (half + half * jnp.tanh(half)).astype(jnp.bfloat16)


def network_kernel(plan, blocks, groups, *refs):
    block_refs = refs[:blocks]
    w1_ref, mid_ref, wo_ref, state_ref, out_ref, wide_ref, tile_ref, sum_ref, sems = refs[blocks:]
    features = plan.nf * plan.levs
    rows = features * plan.lon_dev
    for s, ref in enumerate(block_refs):
        wide_ref[s * rows : (s + 1) * rows, :] = ref[...].astype(jnp.float32)
    copies = []
    for number, (start, stop) in enumerate(groups):
        inputs = jnp.concatenate(
            [
                wide_ref[pl.ds(lon, blocks * features, stride=plan.lon_dev), :].astype(jnp.bfloat16)
                for lon in range(start, stop)
            ],
            axis=1,
        )
        hidden = silu_of_half(mm(w1_ref[...], inputs))
        hidden = silu_of_half(mm(mid_ref[0], hidden))
        hidden = silu_of_half(mm(mid_ref[1], hidden))
        output = mm(wo_ref[...], hidden).astype(jnp.bfloat16).astype(jnp.float32)
        for lon in range(start, stop):
            tile_ref[lon] = output[:, (lon - start) * plan.lat_dev : (lon - start + 1) * plan.lat_dev]
        for f in range(plan.nf):
            for l in range(plan.levs):
                correction = tile_ref[start:stop, f * plan.levs + l, :]
                sum_ref[f, start:stop, l, :] = state_ref[f, l, start:stop, :] + correction
            part = (f, pl.ds(start, stop - start))
            copy = pltpu.make_async_copy(sum_ref.at[part], out_ref.at[part], sems.at[number, f])
            copy.start()
            copies.append(copy)
    for copy in copies:
        copy.wait()


def network(plan, state, blocks, weights):
    vmem = pl.BlockSpec(memory_space=pltpu.VMEM)
    size = max(1, GROUP // plan.lat_dev)
    groups = [(start, min(start + size, plan.lon_dev)) for start in range(0, plan.lon_dev, size)]
    out = jax.ShapeDtypeStruct((plan.nf, plan.lon_dev, plan.levs, plan.lat_dev), jnp.float32)
    return pl.pallas_call(
        functools.partial(network_kernel, plan, len(blocks), groups),
        out_shape=out,
        in_specs=[vmem] * (len(blocks) + 4),
        out_specs=pl.BlockSpec(memory_space=pltpu.HBM),
        scratch_shapes=[
            pltpu.VMEM((round_up(len(blocks) * plan.nf * plan.levs * plan.lon_dev, 8) + 8, plan.lat_dev), jnp.float32),
            pltpu.VMEM((plan.lon_dev, plan.feats, plan.lat_dev), jnp.float32),
            pltpu.VMEM(out.shape, jnp.float32),
            pltpu.SemaphoreType.DMA((len(groups), plan.nf)),
        ],
        compiler_params=pltpu.CompilerParams(vmem_limit_bytes=24 * 1024 * 1024),
        name="network",
    )(*blocks, *weights, state)


def swap(value, axes, sizes, mask):
    count = int(np.prod(sizes))
    return lax.ppermute(value, axes, [(i, i ^ mask) for i in range(count)])


def gathering(plan, fields, spectral_coeffs, mlp_in, mlp_mid, mlp_out):
    fields = fields.transpose(0, 2, 1, 3)
    plane = ("lon", "lat")
    sizes = (plan.lons, plan.lats)
    blocks = [None] * (plan.lons * plan.lats)
    outer = [(lon, lat) for lat in range(0, plan.lats, 2) for lon in range(plan.lons)]
    for lon, lat in outer:
        mask = lon * plan.lats + lat
        blocks[lat * plan.lons + lon] = swap(fields, plane, sizes, mask) if mask else fields
    if plan.lats > 1:
        for lon, lat in outer:
            blocks[(lat ^ 1) * plan.lons + lon] = swap(blocks[lat * plan.lons + lon], plane, sizes, 1)
    sums, tables = prepare(plan, spectral_coeffs.T)
    weights = order_weights(plan, mlp_in.T, mlp_mid, mlp_out)
    state, feats = dynamics(plan, blocks, tables, sums)
    parts = [feats]
    for mask in range(1, plan.zs):
        parts.append(swap(feats, ("lev",), (plan.zs,), mask))
    return network(plan, state, parts, weights).transpose(0, 2, 1, 3)


def solution(mesh):
    in_specs = (P(None, "lev", "lon", "lat"), P(None, "lev"), P(), P(), P())
    out_specs = P(None, "lev", "lon", "lat")

    def per_device(fields, spectral_coeffs, mlp_in, mlp_mid, mlp_out):
        plan = Plan(mesh.shape, fields.shape)
        if plan.fits():
            return gathering(plan, fields, spectral_coeffs, mlp_in, mlp_mid, mlp_out)
        return transposing(fields, spectral_coeffs, mlp_in, mlp_mid, mlp_out)

    def step(fields, *rest):
        return jax.shard_map(
            per_device, mesh=mesh, in_specs=in_specs, out_specs=out_specs, check_vma=False
        )(fields, *rest)

    return step
```

```python
import functools

import jax
import jax.numpy as jnp
import numpy as np
from jax import lax
from jax.experimental import pallas as pl
from jax.experimental.pallas import tpu as pltpu
from jax.sharding import PartitionSpec as P


WAVES = 320
KMAX = 320
SUBSTEPS = 2


highest = lax.Precision.HIGHEST
LANES = 128
GROUP = 2048
PLANE_LIMIT = 4 * 1024 * 1024


def round_up(value, unit):
    return -(-value // unit) * unit


def forward_table(lon_ids, total_lon, waves):
    wave_ids = jnp.arange(waves, dtype=jnp.int32)
    phase = (lon_ids[:, None] * wave_ids[None, :] % total_lon).astype(jnp.float32) * (
        2.0 * jnp.pi / total_lon
    )
    return jnp.concatenate([jnp.cos(phase), -jnp.sin(phase)], axis=1) / total_lon


def inverse_table(lon_ids, total_lon, waves):
    wave_ids = jnp.arange(waves, dtype=jnp.int32)
    phase = (wave_ids[:, None] * lon_ids[None, :] % total_lon).astype(jnp.float32) * (
        2.0 * jnp.pi / total_lon
    )
    weight = jnp.where(wave_ids == 0, 1.0, 2.0).astype(jnp.float32)[:, None]
    return jnp.concatenate([weight * jnp.cos(phase), -weight * jnp.sin(phase)], axis=0)


def latitude_tables(lat_ids, total_lat, degree_ids):
    odd_rows = 2 * lat_ids[:, None] + 1
    period = 4 * total_lat
    scale = jnp.pi / (2.0 * total_lat)
    even_arg = (odd_rows * degree_ids[None, :] % period).astype(jnp.float32) * scale
    odd_arg = (odd_rows * (degree_ids[None, :] + 1) % period).astype(jnp.float32) * scale
    return (jnp.cos(even_arg), jnp.sin(odd_arg))


def latitude_forward(waves, even_tab, odd_tab):
    cols, nf, levs, lats = waves.shape
    pairs = waves.reshape(cols // 2, 2, nf, levs, lats)
    even_part = jnp.einsum("pfli,ik->pflk", pairs[:, 0], even_tab, precision=highest)
    odd_part = jnp.einsum("pfli,ik->pflk", pairs[:, 1], odd_tab, precision=highest)
    return jnp.stack([even_part, odd_part], axis=1).reshape(cols, nf, levs, even_tab.shape[1])


def latitude_inverse(spectra, even_tab, odd_tab):
    cols, nf, levs, degs = spectra.shape
    pairs = spectra.reshape(cols // 2, 2, nf, levs, degs)
    even_part = jnp.einsum("pflk,ik->pfli", pairs[:, 0], even_tab, precision=highest)
    odd_part = jnp.einsum("pflk,ik->pfli", pairs[:, 1], odd_tab, precision=highest)
    return jnp.stack([even_part, odd_part], axis=1).reshape(cols, nf, levs, even_tab.shape[0])


def operator(spectra, coeffs, col_waves, degree_ids):
    parity = col_waves % 2
    freq = (degree_ids[None, :] + parity[:, None]).astype(jnp.float32)
    wavenum = col_waves.astype(jnp.float32)[:, None]
    qvalue = ((wavenum * wavenum + freq * freq) / (KMAX * KMAX))[:, None, :]
    hyper = coeffs[0][None, :, None]
    coupling = coeffs[1][None, :, None]
    depth = coeffs[2][None, :, None]
    vort = spectra[:, 0]
    diverg = spectra[:, 1]
    temper = spectra[:, 2]
    new_vort = vort / (1.0 + hyper * qvalue * qvalue)
    new_div = (diverg + coupling * qvalue * temper) / (1.0 + coupling * depth * qvalue)
    new_temp = temper - depth * new_div
    return jnp.stack([new_vort - vort, new_div - diverg, new_temp - temper], axis=1)


def nonlinear(state):
    temper = state[2] + 0.25 * state[0] * state[1]
    return jnp.stack([state[0], state[1], temper], axis=0)


def transposing(fields, spectral_coeffs, mlp_in, mlp_mid, mlp_out):
    nf, lev_dev, lon_dev, lat_dev = fields.shape
    lon_count = lax.axis_size("lon")
    lat_count = lax.axis_size("lat")
    total_lon = lon_dev * lon_count
    total_lat = lat_dev * lat_count
    wave_cols = 2 * WAVES // lon_count
    row_count = nf * lev_dev * lat_dev
    lat_ids = lax.axis_index("lat") * lat_dev + jnp.arange(lat_dev, dtype=jnp.int32)
    col_waves = (lax.axis_index("lon") * wave_cols + jnp.arange(wave_cols, dtype=jnp.int32)) % WAVES
    weight = 2.0 / total_lat
    all_lons = jnp.arange(total_lon, dtype=jnp.int32)
    fwd_full = forward_table(all_lons, total_lon, WAVES)
    inv_full = inverse_table(all_lons, total_lon, WAVES)
    own_degrees = jnp.arange(KMAX, dtype=jnp.int32)
    full_even, full_odd = latitude_tables(lat_ids, total_lat, own_degrees)
    state = fields
    for _ in range(SUBSTEPS):
        flat = state.transpose(0, 1, 3, 2).reshape(row_count, lon_dev)
        by_row = lax.all_to_all(flat, "lon", split_axis=0, concat_axis=1, tiled=True)
        row_waves = jnp.dot(by_row, fwd_full, precision=highest)
        by_col = lax.all_to_all(row_waves, "lon", split_axis=1, concat_axis=0, tiled=True)
        waves = by_col.reshape(nf, lev_dev, lat_dev, wave_cols).transpose(3, 0, 1, 2)
        partial_spectra = latitude_forward(waves, full_even * weight, full_odd * weight)
        spectra = lax.psum(partial_spectra, "lat")
        change = operator(spectra, spectral_coeffs, col_waves, own_degrees)
        back = latitude_inverse(change, full_even, full_odd)
        flat_back = back.transpose(1, 2, 3, 0).reshape(row_count, wave_cols)
        full_waves = lax.all_to_all(flat_back, "lon", split_axis=0, concat_axis=1, tiled=True)
        row_grid = jnp.dot(full_waves, inv_full, precision=highest)
        own_grid = lax.all_to_all(row_grid, "lon", split_axis=1, concat_axis=0, tiled=True)
        increment = own_grid.reshape(nf, lev_dev, lat_dev, lon_dev).transpose(0, 1, 3, 2)
        state = nonlinear(state + increment)
    features = state.astype(jnp.bfloat16).reshape(nf, lev_dev, lon_dev * lat_dev)
    columns = lax.all_to_all(features, "lev", split_axis=2, concat_axis=1, tiled=True)
    levels = columns.shape[1]
    inputs = columns.reshape(nf * levels, columns.shape[2])
    hidden = jax.nn.silu(jnp.dot(mlp_in, inputs, preferred_element_type=jnp.float32)).astype(
        jnp.bfloat16
    )
    hidden = jax.nn.silu(jnp.dot(mlp_mid[0], hidden, preferred_element_type=jnp.float32)).astype(
        jnp.bfloat16
    )
    hidden = jax.nn.silu(jnp.dot(mlp_mid[1], hidden, preferred_element_type=jnp.float32)).astype(
        jnp.bfloat16
    )
    output = jnp.dot(mlp_out, hidden, preferred_element_type=jnp.float32).astype(jnp.bfloat16)
    output = output.reshape(nf, levels, columns.shape[2])
    returned = lax.all_to_all(output, "lev", split_axis=1, concat_axis=2, tiled=True)
    return state + returned.astype(jnp.float32).reshape(state.shape)


class Plan:
    def __init__(self, mesh_shape, local):
        self.nf, self.levs, self.lon_dev, self.lat_dev = local
        self.lons = mesh_shape["lon"]
        self.lats = mesh_shape["lat"]
        self.zs = mesh_shape["lev"]
        self.n_lon = self.lons * self.lon_dev
        self.n_lat = self.lats * self.lat_dev
        self.jpad = round_up(self.lon_dev, 16)
        self.rows = self.lons * self.jpad
        classes = min(self.n_lon // 2 + 1, WAVES)
        self.half = round_up((classes + 1) // 2, 16)
        self.block = 2 * self.half
        self.modes = 2 * self.block
        self.degs = round_up(-(-KMAX // 2), 16)
        self.side = self.lats // 2
        self.feats = round_up(self.nf * self.levs, 8)

    def fits(self):
        plane = self.nf * self.levs * self.n_lon * self.n_lat * 4
        power_of_two = all(n & (n - 1) == 0 for n in (self.lons, self.lats, self.zs))
        return (
            SUBSTEPS == 2
            and self.nf == 3
            and power_of_two
            and plane <= PLANE_LIMIT
            and self.n_lon % 2 == 0
            and self.lats % 2 == 0
            and self.lat_dev == LANES
            and KMAX < self.n_lat
        )


def split_np(table):
    high = table.astype(np.float32).astype(jnp.bfloat16)
    low = (table - high.astype(np.float64)).astype(jnp.bfloat16)
    return high, low


def zonal_tables(plan):
    lon = np.arange(plan.n_lon)
    pos = (lon // plan.lon_dev) * plan.jpad + lon % plan.lon_dev
    scale = 2.0 / (plan.n_lon * plan.n_lat)
    ana = np.zeros((plan.modes, plan.rows))
    syn = np.zeros((plan.rows, plan.modes))
    classes = min(plan.n_lon // 2 + 1, WAVES)
    for rho in range(classes):
        phase = 2.0 * np.pi * ((rho * lon) % plan.n_lon) / plan.n_lon
        cos_row = (rho % 2) * plan.block + rho // 2
        ana[cos_row, pos] = scale * np.cos(phase)
        syn[pos, cos_row] = np.cos(phase)
        if rho > 0 and 2 * rho != plan.n_lon:
            ana[cos_row + plan.half, pos] = -scale * np.sin(phase)
            syn[pos, cos_row + plan.half] = -np.sin(phase)
    ana_h, ana_l = split_np(ana)
    syn_h, syn_l = split_np(syn)
    return (
        np.concatenate([ana_h, ana_l, ana_h], axis=1),
        np.concatenate([syn_h, syn_l, syn_h], axis=1),
    )


def meridional_tables(plan):
    lat = np.arange(plan.n_lat // 2)[None, :]
    deg = np.arange(KMAX)[:, None]
    period = 4 * plan.n_lat
    scale = np.pi / (2.0 * plan.n_lat)
    even = np.cos(((2 * lat + 1) * deg % period) * scale)
    odd = np.sin(((2 * lat + 1) * (deg + 1) % period) * scale)
    out = np.zeros((2, 2, 2, plan.degs, plan.n_lat // 2), dtype=jnp.bfloat16)
    for parity, table in enumerate((even, odd)):
        for kind in range(2):
            for part, value in enumerate(split_np(table[kind::2])):
                out[parity, kind, part, : value.shape[0]] = value
    return out


def split(value):
    high = value.astype(jnp.bfloat16)
    low = (value - high.astype(jnp.float32)).astype(jnp.bfloat16)
    return high, low


def mm(left, right):
    return lax.dot_general(
        left, right, (((1,), (0,)), ((), ())), preferred_element_type=jnp.float32
    )


def mm_l(left, right):
    return lax.dot_general(
        left, right, (((0,), (0,)), ((), ())), preferred_element_type=jnp.float32
    )


def mm_t(left, right):
    return lax.dot_general(
        left, right, (((1,), (1,)), ((), ())), preferred_element_type=jnp.float32
    )


def prepare_kernel(plan, coef_hbm, *refs):
    sources, refs = refs[:3], refs[3:]
    sv_ref, sq_ref, count_ref, gb_ref = refs[:4]
    targets, (coef_ref, sems) = refs[4:7], refs[7:]
    first = pltpu.make_async_copy(coef_hbm, coef_ref, sems.at[3])
    first.start()
    copies = [pltpu.make_async_copy(source, target, sems.at[n]) for n, (source, target) in enumerate(zip(sources, targets))]
    for copy in copies:
        copy.start()
    first.wait()
    for lev in range(plan.levs):
        gb_ref[lev] = jnp.full(gb_ref.shape[1:], coef_ref[lev, 2], jnp.float32)
    row = lax.broadcasted_iota(jnp.int32, (plan.half, plan.degs), 0)
    lane = lax.broadcasted_iota(jnp.int32, (plan.half, plan.degs), 1)
    inv_k2 = 1.0 / (KMAX * KMAX)
    turns = -(-WAVES // plan.n_lon)
    for parity in range(2):
        rho = 2 * row + parity
        terms = []
        for turn in range(turns):
            wave = rho + plan.n_lon * turn
            terms.append((wave, (wave < WAVES) & (2 * rho <= plan.n_lon)))
            wave = plan.n_lon * (turn + 1) - rho
            terms.append((wave, (wave < WAVES) & (rho > 0) & (2 * rho < plan.n_lon)))
        terms = [
            (wave.astype(jnp.float32), jnp.where(valid, jnp.where(wave == 0, 1.0, 2.0), 0.0)) for wave, valid in terms
        ]
        count_ref[parity] = sum(weight for _, weight in terms)
        for kind in range(2):
            freq = (2 * lane + kind + parity).astype(jnp.float32)
            freq2 = freq * freq
            sums = [[jnp.zeros((plan.half, plan.degs), jnp.float32) for _ in range(2)] for _ in range(plan.levs)]
            for wave, weight in terms:
                q = (wave * wave + freq2) * inv_k2
                for lev in range(plan.levs):
                    nu, ga, gb = (coef_ref[lev, i] for i in range(3))
                    hyper = nu * q * q
                    wave_q = ga * q
                    sums[lev][0] -= weight * (hyper / (1.0 + hyper))
                    sums[lev][1] += weight * (wave_q / (1.0 + gb * wave_q))
            for lev in range(plan.levs):
                sv_ref[lev, parity, kind] = sums[lev][0]
                sq_ref[lev, parity, kind] = sums[lev][1]
    for copy in copies:
        copy.wait()


def prepare(plan, coeffs):
    table = jax.ShapeDtypeStruct((plan.levs, 2, 2, plan.half, plan.degs), jnp.float32)
    vmem = pl.BlockSpec(memory_space=pltpu.VMEM)
    tables = [jnp.asarray(t) for t in (*zonal_tables(plan), meridional_tables(plan))]
    out = pl.pallas_call(
        functools.partial(prepare_kernel, plan),
        out_shape=(
            table,
            table,
            jax.ShapeDtypeStruct((2, plan.half, plan.degs), jnp.float32),
            jax.ShapeDtypeStruct((plan.levs, 8, LANES), jnp.float32),
            *(jax.ShapeDtypeStruct(t.shape, t.dtype) for t in tables),
        ),
        in_specs=[pl.BlockSpec(memory_space=pltpu.HBM)] * (1 + len(tables)),
        out_specs=(vmem,) * (4 + len(tables)),
        scratch_shapes=[pltpu.SMEM(coeffs.shape, jnp.float32), pltpu.SemaphoreType.DMA((1 + len(tables),))],
        compiler_params=pltpu.CompilerParams(vmem_limit_bytes=16 * 1024 * 1024),
        name="prepare",
    )(*[pltpu.with_memory_space_constraint(t, pltpu.HBM) for t in (coeffs, *tables)])
    return out[:4], out[4:]


def weights_kernel(plan, win_ref, mid_ref, wout_ref, w1_ref, half_ref, wo_ref):
    half_ref[...] = (0.5 * mid_ref[...].astype(jnp.float32)).astype(jnp.bfloat16)
    own_z = lax.axis_index("lev")
    total = plan.zs * plan.levs
    nin = plan.nf * total

    def feature_of(slot, count):
        block = slot // count
        inner = slot % count
        field = inner // plan.levs
        level = (own_z ^ block) * plan.levs + inner % plan.levs
        return jnp.where(inner < plan.nf * plan.levs, field * total + level, -1)

    count = plan.nf * plan.levs
    wide = plan.zs * count
    source = lax.broadcasted_iota(jnp.int32, (nin, wide), 0)
    slot = lax.broadcasted_iota(jnp.int32, (nin, wide), 1)
    pick = (source == feature_of(slot, count)).astype(jnp.float32).astype(jnp.bfloat16)
    w1_ref[...] = (0.5 * mm_l(win_ref[...], pick)).astype(jnp.bfloat16)
    slot = lax.broadcasted_iota(jnp.int32, (plan.feats, nin), 0)
    source = lax.broadcasted_iota(jnp.int32, (plan.feats, nin), 1)
    pick = (source == feature_of(slot, plan.feats)).astype(jnp.float32).astype(jnp.bfloat16)
    wo_ref[...] = mm(pick, wout_ref[...]).astype(jnp.bfloat16)


def order_weights(plan, mlp_in, mlp_mid, mlp_out):
    units = mlp_in.shape[1]
    vmem = pl.BlockSpec(memory_space=pltpu.VMEM)
    return pl.pallas_call(
        functools.partial(weights_kernel, plan),
        out_shape=(
            jax.ShapeDtypeStruct((units, plan.zs * plan.nf * plan.levs), jnp.bfloat16),
            jax.ShapeDtypeStruct(mlp_mid.shape, jnp.bfloat16),
            jax.ShapeDtypeStruct((plan.feats, units), jnp.bfloat16),
        ),
        in_specs=[vmem] * 3,
        out_specs=(vmem,) * 3,
        compiler_params=pltpu.CompilerParams(vmem_limit_bytes=16 * 1024 * 1024),
        name="order_weights",
    )(mlp_in, mlp_mid, mlp_out)


def dynamics_kernel(plan, blocks, *refs):
    block_refs = refs[:blocks]
    ana_ref, syn_ref, mer_ref, sv_ref, sq_ref, count_ref, gb_ref = refs[blocks : 7 + blocks]
    state_ref, feat_ref = refs[7 + blocks : 9 + blocks]
    grid_ref, prod_ref, pack_ref = refs[9 + blocks :]
    own_lon, own_lat = lax.axis_index("lon"), lax.axis_index("lat")
    nf, levs, lats = plan.nf, plan.levs, plan.lats
    block, half = plan.block, plan.half
    if plan.jpad != plan.lon_dev:
        tail = (plan.lon_dev // 8) * 8
        for lon in range(plan.lons):
            start = lon * plan.jpad + tail
            stop = (lon + 1) * plan.jpad
            zeros = jnp.zeros((stop - start, plan.lat_dev), jnp.float32)
            for side in range(2):
                for lat in range(plan.side):
                    for f in range(nf):
                        for l in range(levs):
                            grid_ref[side, lat, f, l, start:stop, :] = zeros

    def place(lat):
        south = lat >= plan.side
        return jnp.where(south, 1, 0), jnp.where(south, lats - 1 - lat, lat)

    def mirror(value, side):
        lane = lax.broadcasted_iota(jnp.int32, value.shape, 1)
        lane = jnp.where(side == 1, plan.lat_dev - 1 - lane, lane)
        return jnp.take_along_axis(value, lane, axis=1, mode="promise_in_bounds")

    for s in range(blocks):
        lon = own_lon ^ (s % plan.lons)
        side, lat = place(own_lat ^ (s // plan.lons))
        row = pl.multiple_of(lon * plan.jpad, 8)
        for f in range(nf):
            for l in range(levs):
                value = block_refs[s][f, :, l, :]
                grid_ref[side, lat, f, l, pl.ds(row, plan.lon_dev), :] = mirror(value, side)

    def whole(ref, side, *index):
        return jnp.concatenate([ref[(side, lat, *index)] for lat in range(plan.side)], axis=1)

    def analyse(values):
        middle = plan.n_lat // 2
        parts = []
        for north, south in values:
            high, low = split(jnp.concatenate([north + south, north - south], axis=1))
            parts.append(split(mm(ana_ref[...], jnp.concatenate([high, high, low], axis=0))))
        out = []
        for parity in range(2):
            kinds = []
            for kind in range(2):
                lanes = slice(kind * middle, (kind + 1) * middle)
                rows = slice(parity * block, (parity + 1) * block)
                high, low = (jnp.concatenate([part[n][rows, lanes] for part in parts], axis=0) for n in range(2))
                thigh, tlow = mer_ref[parity, kind, 0], mer_ref[parity, kind, 1]
                count = high.shape[0]
                tall = mm_t(jnp.concatenate([high, low], axis=0), thigh)
                kinds.append(tall[:count] + tall[count:] + mm_t(high, tlow))
            out.append(kinds)
        return out

    def synthesise(spectra, rows, table):
        parts = []
        for parity in range(2):
            kinds = []
            for kind in range(2):
                high, low = split(spectra[parity][kind])
                thigh, tlow = table(parity, kind)
                size = thigh.shape[1]
                if size <= LANES:
                    wide = mm(high, jnp.concatenate([thigh, tlow], axis=1))
                    kinds.append(wide[:, :size] + wide[:, size:] + mm(low, thigh))
                else:
                    kinds.append(mm(high, thigh) + mm(low, thigh) + mm(high, tlow))
            parts.append(jnp.concatenate(kinds, axis=1))
        count = spectra[0][0].shape[0] // block
        width = parts[0].shape[1] // 2
        out = []
        for n in range(count):
            both = jnp.concatenate([part[n * block : (n + 1) * block] for part in parts], axis=0)
            high, low = split(both)
            grid = mm(rows, jnp.concatenate([high, high, low], axis=0))
            out.append((grid[:, :width], grid[:, width:]))
        return out

    def at(spectrum, f, l):
        n = f * levs + l
        return spectrum[n * block : (n + 1) * block]

    pairs = [(parity, kind) for parity in range(2) for kind in range(2)]
    lane = lax.broadcasted_iota(jnp.int32, (block, plan.degs), 1)
    cls = lax.broadcasted_iota(jnp.int32, (block, plan.degs), 0) % half
    norms, counts = {}, {}
    for parity in range(2):
        rho = 2 * cls + parity
        alone = (rho == 0) | (2 * rho == plan.n_lon)
        norm = jnp.where(alone, 1.0, 0.5)
        weight = jnp.concatenate([count_ref[parity]] * 2, axis=0)
        for kind in range(2):
            counts[parity, kind] = weight
            norms[parity, kind] = norm * jnp.where(lane == 0, 2.0, 1.0) if parity == kind == 0 else norm

    def changes(spectra):
        out = {}
        for pair in pairs:
            per = [[None] * levs for _ in range(nf)]
            for l in range(levs):
                sv = jnp.concatenate([sv_ref[(l, *pair)]] * 2, axis=0)
                sq = jnp.concatenate([sq_ref[(l, *pair)]] * 2, axis=0)
                gb = gb_ref[l, 0:1, 0:1]
                vort, diverg, temper = (spectra[pair][f][l] for f in range(3))
                per[0][l] = sv * vort
                per[1][l] = sq * (temper - gb * diverg)
                per[2][l] = -gb * (counts[pair] * diverg + per[1][l])
            out[pair] = per
        return out

    def stack(nested, fields):
        return [
            [
                jnp.concatenate([nested[parity, kind][f][l] for f in fields for l in range(levs)], axis=0)
                for kind in range(2)
            ]
            for parity in range(2)
        ]

    flat = analyse([tuple(whole(grid_ref, side, f, l) for side in range(2)) for f in range(nf) for l in range(levs)])
    spectra = {
        (parity, kind): [[at(flat[parity][kind], f, l) for l in range(levs)] for f in range(nf)]
        for parity, kind in pairs
    }
    first = changes(spectra)
    grown = synthesise(
        stack(first, (0, 1)), syn_ref[...], lambda parity, kind: (mer_ref[parity, kind, 0], mer_ref[parity, kind, 1])
    )
    products = []
    for l in range(levs):
        (vsym, vanti), (dsym, danti) = grown[l], grown[levs + l]
        sides = []
        for side in range(2):
            vort = whole(grid_ref, side, 0, l) + (vsym - vanti if side else vsym + vanti)
            diverg = whole(grid_ref, side, 1, l) + (dsym - danti if side else dsym + danti)
            product = 0.25 * vort * diverg
            for lat in range(plan.side):
                prod_ref[side, lat, l] = product[:, lat * plan.lat_dev : (lat + 1) * plan.lat_dev]
            sides.append(product)
        products.append(tuple(sides))
    extra = analyse(products)
    updated = {}
    for pair in pairs:
        per = [[spectra[pair][f][l] + norms[pair] * first[pair][f][l] for l in range(levs)] for f in range(nf)]
        per[2] = [per[2][l] + at(extra[pair[0]][pair[1]], 0, l) for l in range(levs)]
        updated[pair] = per
    second = changes(updated)
    both = {
        pair: [[first[pair][f][l] + second[pair][f][l] for l in range(levs)] for f in range(nf)] for pair in pairs
    }
    side, lat = place(own_lat)
    own_start = pl.multiple_of(lat * plan.lat_dev, LANES)
    own_row = pl.multiple_of(own_lon * plan.jpad, 8)
    own = synthesise(
        stack(both, range(nf)),
        syn_ref[pl.ds(own_row, plan.jpad), :],
        lambda parity, kind: tuple(mer_ref[parity, kind, part, :, pl.ds(own_start, plan.lat_dev)] for part in range(2)),
    )
    sign = jnp.where(side == 1, -1.0, 1.0)
    for l in range(levs):
        vort, diverg, temper = (
            grid_ref[side, lat, f, l, pl.ds(own_row, plan.jpad), :]
            + (own[f * levs + l][0] + sign * own[f * levs + l][1])
            for f in range(3)
        )
        temper = temper + prod_ref[side, lat, l, pl.ds(own_row, plan.jpad), :] + 0.25 * vort * diverg
        for f, value in enumerate((vort, diverg, temper)):
            value = mirror(value, side)
            state_ref[f, l] = value[: plan.lon_dev]
            start = (f * levs + l) * plan.lon_dev
            pack_ref[start : start + plan.lon_dev, :] = value[: plan.lon_dev]
    feat_ref[...] = pack_ref[: feat_ref.shape[0], :].astype(jnp.bfloat16)


def dynamics(plan, blocks, tables, sums):
    vmem = pl.BlockSpec(memory_space=pltpu.VMEM)
    return pl.pallas_call(
        functools.partial(dynamics_kernel, plan, len(blocks)),
        out_shape=(
            jax.ShapeDtypeStruct((plan.nf, plan.levs, plan.lon_dev, plan.lat_dev), jnp.float32),
            jax.ShapeDtypeStruct((plan.nf * plan.levs * plan.lon_dev, plan.lat_dev), jnp.bfloat16),
        ),
        in_specs=[vmem] * (len(blocks) + 7),
        out_specs=(vmem,) * 2,
        scratch_shapes=[
            pltpu.VMEM((2, plan.side, plan.nf, plan.levs, plan.rows, plan.lat_dev), jnp.float32),
            pltpu.VMEM((2, plan.side, plan.levs, plan.rows, plan.lat_dev), jnp.float32),
            pltpu.VMEM((round_up(plan.nf * plan.levs * plan.lon_dev, 8) + 8, plan.lat_dev), jnp.float32),
        ],
        compiler_params=pltpu.CompilerParams(vmem_limit_bytes=32 * 1024 * 1024),
        name="dynamics",
    )(*blocks, *tables, *sums)


def silu_of_half(half):
    return (half + half * jnp.tanh(half)).astype(jnp.bfloat16)


def network_kernel(plan, blocks, groups, *refs):
    block_refs = refs[:blocks]
    w1_ref, mid_ref, wo_ref, state_ref, out_ref, wide_ref, tile_ref, sum_ref, sems = refs[blocks:]
    features = plan.nf * plan.levs
    rows = features * plan.lon_dev
    for s, ref in enumerate(block_refs):
        wide_ref[s * rows : (s + 1) * rows, :] = ref[...].astype(jnp.float32)
    copies = []
    for number, (start, stop) in enumerate(groups):
        inputs = jnp.concatenate(
            [
                wide_ref[pl.ds(lon, blocks * features, stride=plan.lon_dev), :].astype(jnp.bfloat16)
                for lon in range(start, stop)
            ],
            axis=1,
        )
        hidden = silu_of_half(mm(w1_ref[...], inputs))
        hidden = silu_of_half(mm(mid_ref[0], hidden))
        hidden = silu_of_half(mm(mid_ref[1], hidden))
        output = mm(wo_ref[...], hidden).astype(jnp.bfloat16).astype(jnp.float32)
        for lon in range(start, stop):
            tile_ref[lon] = output[:, (lon - start) * plan.lat_dev : (lon - start + 1) * plan.lat_dev]
        for f in range(plan.nf):
            for l in range(plan.levs):
                correction = tile_ref[start:stop, f * plan.levs + l, :]
                sum_ref[f, start:stop, l, :] = state_ref[f, l, start:stop, :] + correction
        part = (slice(None), pl.ds(start, stop - start))
        copy = pltpu.make_async_copy(sum_ref.at[part], out_ref.at[part], sems.at[number])
        copy.start()
        copies.append(copy)
    for copy in copies:
        copy.wait()


def network(plan, state, blocks, weights):
    vmem = pl.BlockSpec(memory_space=pltpu.VMEM)
    size = max(1, GROUP // plan.lat_dev)
    groups = [(start, min(start + size, plan.lon_dev)) for start in range(0, plan.lon_dev, size)]
    out = jax.ShapeDtypeStruct((plan.nf, plan.lon_dev, plan.levs, plan.lat_dev), jnp.float32)
    return pl.pallas_call(
        functools.partial(network_kernel, plan, len(blocks), groups),
        out_shape=out,
        in_specs=[vmem] * (len(blocks) + 4),
        out_specs=pl.BlockSpec(memory_space=pltpu.HBM),
        scratch_shapes=[
            pltpu.VMEM((round_up(len(blocks) * plan.nf * plan.levs * plan.lon_dev, 8) + 8, plan.lat_dev), jnp.float32),
            pltpu.VMEM((plan.lon_dev, plan.feats, plan.lat_dev), jnp.float32),
            pltpu.VMEM(out.shape, jnp.float32),
            pltpu.SemaphoreType.DMA((len(groups),)),
        ],
        compiler_params=pltpu.CompilerParams(vmem_limit_bytes=24 * 1024 * 1024),
        name="network",
    )(*blocks, *weights, state)


def swap(value, axes, sizes, mask):
    count = int(np.prod(sizes))
    return lax.ppermute(value, axes, [(i, i ^ mask) for i in range(count)])


def gathering(plan, fields, spectral_coeffs, mlp_in, mlp_mid, mlp_out):
    fields = fields.transpose(0, 2, 1, 3)
    plane = ("lon", "lat")
    sizes = (plan.lons, plan.lats)
    blocks = [None] * (plan.lons * plan.lats)
    outer = [(lon, lat) for lat in range(0, plan.lats, 2) for lon in range(plan.lons)]
    for lon, lat in outer:
        mask = lon * plan.lats + lat
        blocks[lat * plan.lons + lon] = swap(fields, plane, sizes, mask) if mask else fields
    if plan.lats > 1:
        for lon, lat in outer:
            blocks[(lat ^ 1) * plan.lons + lon] = swap(blocks[lat * plan.lons + lon], plane, sizes, 1)
    sums, tables = prepare(plan, spectral_coeffs.T)
    weights = order_weights(plan, mlp_in.T, mlp_mid, mlp_out)
    state, feats = dynamics(plan, blocks, tables, sums)
    parts = [feats]
    for mask in range(1, plan.zs):
        parts.append(swap(feats, ("lev",), (plan.zs,), mask))
    return network(plan, state, parts, weights).transpose(0, 2, 1, 3)


def solution(mesh):
    in_specs = (P(None, "lev", "lon", "lat"), P(None, "lev"), P(), P(), P())
    out_specs = P(None, "lev", "lon", "lat")

    def per_device(fields, spectral_coeffs, mlp_in, mlp_mid, mlp_out):
        plan = Plan(mesh.shape, fields.shape)
        if plan.fits():
            return gathering(plan, fields, spectral_coeffs, mlp_in, mlp_mid, mlp_out)
        return transposing(fields, spectral_coeffs, mlp_in, mlp_mid, mlp_out)

    def step(fields, *rest):
        return jax.shard_map(
            per_device, mesh=mesh, in_specs=in_specs, out_specs=out_specs, check_vma=False
        )(fields, *rest)

    return step
```
